512 devices in a mesh: blk: 8 (over y_lo, x), rows: 64 (over z, y_hi, core).
Axes of the slice: x: 4, y: 4 (y_hi: 2, y_lo: 2; y = y_hi * 2 + y_lo), z: 16, core: 2. Of those that a mesh axis runs over, the one named last changes fastest.
Arguments:
- queries: bfloat16 [128, 4, 8192], P('rows', None, 'blk'), may hold values from -36 to 36
- new_entries: bfloat16 [128, 4, 2, 1024], P('rows', None, None, 'blk'), may hold values from -9 to 9
- resident: bfloat16 [4096, 2, 16, 1024], P('rows', None, None, 'blk'), may hold values from -9 to 9
- swap_area: bfloat16 [4096, 2, 16, 1024], P('rows', None, None, 'blk'), may hold values from -9 to 9
- swap_dest: int32 [4096], P('rows'), may hold values from 0 to 63, as said below
- page_table: int32 [128, 64], P('rows'), may hold values from 0 to 191, as said below
- lengths: int32 [128], P('rows'), may hold values from 256 to 1024, as said below
- norm_gain: bfloat16 [8192], P('blk'), may hold values from 0.099609375 to 1.8984375
- gate_weight: bfloat16 [8192, 28672], P('blk', 'rows'), may hold values from -0.0625 to 0.0625
- up_weight: bfloat16 [8192, 28672], P('blk', 'rows'), may hold values from -0.0625 to 0.0625
- down_weight: bfloat16 [28672, 8192], P('rows', 'blk'), may hold values from -0.03125 to 0.03125
Outputs:
- attended: bfloat16 [128, 4, 8192], P('rows', None, 'blk')
- layer_out: bfloat16 [128, 4, 8192], P('rows', None, 'blk')
The draws below stay inside these ranges and needn't reach their ends.
Inputs may be any that keep to these rules, and one draw needn't show every extreme that they name: `swap_dest`: every owner sends exactly 2 of its pages to each of 32 different owners (possibly itself), and every owner receives exactly 64 pages. `page_table`: the entries of the 2 rows of one owner name each of its 64 resident pages and each of the 64 pages that land there exactly once; an entry at or above 64 is 64 + s * 2 + k for the k-th page, in the order of the sender's pages, that owner s sends to the row's owner. `lengths`: some row has exactly 1024 cached positions.
All inputs are finite; a program needn't handle non-finite values.
Results may differ from the reference program's by a relative error of at most 0.0086.
Values may be sent and summed in bfloat16 or wider, within the bound.
No kernel may reach another device: no remote copies, remote signals or barrier semaphores. Data moves between devices by JAX's collectives and lax.ppermute only.
A program may use at most 64 MiB of HBM per device.

```python
import math
import jax
import jax.numpy as jnp
from jax import lax

KVH = 8
GQ = 8
HD = 128
FF = 28672
PAGE = 16
MAXLEN = 1024
STEPS = 4
CAP = 2
ROWS_DEV = 2
D = 8192
KVD = 1024
MAXPG = 64
OWNERS = 64
SWAP_DEV = 64
RES_DEV = 64
BATCH = 128
N_ROWS = 64


def routing(key):
    base = jax.random.fold_in(key, 11)
    k_sigma, k_tau, k_offset, k_order, k_shuffle = jax.random.split(base, 5)
    sigma = jax.random.permutation(k_sigma, OWNERS)
    tau = jax.random.permutation(k_tau, OWNERS)
    groups = SWAP_DEV // CAP
    offsets = jax.random.permutation(k_offset, OWNERS)[:groups]
    group_dest = sigma[(tau[:, None] + offsets[None, :]) % OWNERS]

    def permute_pages(single):
        return jax.random.permutation(single, SWAP_DEV)
    orders = jax.vmap(permute_pages)(jax.random.split(k_order, OWNERS))
    destination = jnp.take_along_axis(group_dest, orders // CAP, axis=1).astype(jnp.int32)
    target = destination[:, :, None] == jnp.arange(OWNERS, dtype=jnp.int32)[None, None, :]
    before = jnp.cumsum(target.astype(jnp.int32), axis=1) - 1
    ranks = jnp.sum(jnp.where(target, before, 0), axis=2)
    senders = jnp.arange(OWNERS, dtype=jnp.int32)[:, None]
    arrival = destination * (OWNERS * CAP) + senders * CAP + ranks
    ordered = jnp.sort(arrival.reshape(-1)).reshape(OWNERS, SWAP_DEV) % (OWNERS * CAP)
    resident_part = jnp.broadcast_to(jnp.arange(RES_DEV, dtype=jnp.int32)[None, :], (OWNERS, RES_DEV))
    entries = jnp.concatenate([resident_part, RES_DEV + ordered], axis=1)

    def permute_entries(single):
        return jax.random.permutation(single, ROWS_DEV * MAXPG)
    shuffles = jax.vmap(permute_entries)(jax.random.split(k_shuffle, OWNERS))
    entries = jnp.take_along_axis(entries, shuffles, axis=1)
    return (destination.reshape(-1).astype(jnp.int32), entries.reshape(BATCH, MAXPG).astype(jnp.int32))


def draw_swap_dest(key, part):
    return routing(key)[0]


def draw_page_table(key, part):
    return routing(key)[1]


def draw_lengths(key, part):
    drawn = jax.random.randint(jax.random.fold_in(key, 3), (BATCH,), MAXLEN // 4, MAXLEN + 1)
    longest = jax.random.randint(jax.random.fold_in(key, 4), (), 0, BATCH)
    return drawn.at[longest].set(MAXLEN).astype(jnp.int32)


def value_factor():
    rising = 3.0
    head_of = (jnp.arange(KVD) // HD).astype(jnp.float32)
    return 0.5 * rising ** (head_of / (KVH - 1))


def base_values(key, shape):
    return jnp.clip(jax.random.normal(key, shape, jnp.float32), -6.0, 6.0)


def page_values(key, count):
    drawn = base_values(key, (count, 2, PAGE, KVD))
    factors = jnp.stack([jnp.ones((KVD,), jnp.float32), value_factor()])
    return (drawn * factors[None, :, None, :]).astype(jnp.bfloat16)


def draw_resident(key, part):
    return page_values(jax.random.fold_in(key, 5), OWNERS * RES_DEV)


def draw_swap_area(key, part):
    return page_values(jax.random.fold_in(key, 6), OWNERS * SWAP_DEV)


def attention_inputs(key):
    k_query, k_entry = jax.random.split(jax.random.fold_in(key, 23))
    query_draw = base_values(k_query, (BATCH, STEPS, D))
    entry_draw = base_values(k_entry, (BATCH, STEPS, 2, KVD))
    factors = jnp.stack([jnp.ones((KVD,), jnp.float32), value_factor()])
    entry_draw = entry_draw * factors[None, None, :, :]
    return (query_draw.astype(jnp.bfloat16), entry_draw.astype(jnp.bfloat16))


def draw_queries(key, part):
    return attention_inputs(key)[0]


def draw_new_entries(key, part):
    return attention_inputs(key)[1]


def levels(rng, extent, shards, smallest, largest):
    factor_of, own = 1.0, jax.random.fold_in(rng, 6)
    for dim, shards_of in shards:
        heights = jnp.exp(jax.random.uniform(jax.random.fold_in(own, dim), (shards_of,), jnp.float32, smallest / len(shards), largest / len(shards)))
        factor_of = factor_of * jnp.repeat(heights, extent[dim] // shards_of).reshape([-1 if axis == dim else 1 for axis in range(len(extent))])
    return factor_of


def scatter_about(key, shape, width, limit, pieces=(), held_as=jnp.bfloat16):
    values = jax.random.normal(key, shape, jnp.float32) * width
    if len(pieces) > 0:
        values = levels(key, shape, pieces, -0.22, 0.18) * values
    return jnp.clip(values, min=-limit, max=limit).astype(held_as)


def setup_inputs(seed: int = 0) -> dict:
    splits = jax.random.split(jax.random.key(seed), 12)
    return {
        "queries": draw_queries(jax.random.fold_in(splits[11], 71), 0),
        "new_entries": draw_new_entries(jax.random.fold_in(splits[11], 71), 0),
        "resident": draw_resident(jax.random.fold_in(splits[11], 71), 0),
        "swap_area": draw_swap_area(jax.random.fold_in(splits[11], 71), 0),
        "swap_dest": draw_swap_dest(jax.random.fold_in(splits[11], 71), 0),
        "page_table": draw_page_table(jax.random.fold_in(splits[11], 71), 0),
        "lengths": draw_lengths(jax.random.fold_in(splits[11], 71), 0),
        "norm_gain": jnp.clip(1.0 + 0.18 * jax.random.normal(splits[7], (D,), jnp.float32), 0.099609375, 1.8984375).astype(jnp.bfloat16),
        "gate_weight": scatter_about(splits[8], (D, FF), D ** -0.5, 0.0625, ((0, 8), (1, 64))),
        "up_weight": scatter_about(splits[9], (D, FF), D ** -0.5, 0.0625, ((0, 8), (1, 64))),
        "down_weight": scatter_about(splits[10], (FF, D), FF ** -0.5, 0.03125, ((0, 64), (1, 8))),
    }


epsilon = 1e-05

def send_ranks(swap_dest):
    destination = swap_dest.reshape(N_ROWS, SWAP_DEV)
    target = destination[:, :, None] == jnp.arange(N_ROWS, dtype=jnp.int32)[None, None, :]
    before = jnp.cumsum(target.astype(jnp.int32), axis=1) - 1
    return (destination, lax.optimization_barrier(jnp.sum(jnp.where(target, before, 0), axis=2)).astype(jnp.int32))

def reference(queries, new_entries, resident, swap_area, swap_dest, page_table, lengths, norm_gain, gate_weight, up_weight, down_weight):
    destination, ranks = send_ranks(swap_dest)
    senders = jnp.arange(N_ROWS, dtype=jnp.int32)[:, None]
    arrival = (destination * (N_ROWS * CAP) + senders * CAP + ranks).reshape(-1)
    landing = jnp.zeros((N_ROWS * N_ROWS * CAP,), jnp.int32).at[arrival].set(jnp.arange(N_ROWS * SWAP_DEV, dtype=jnp.int32))
    owner = (jnp.arange(BATCH, dtype=jnp.int32) // ROWS_DEV)[:, None]
    resident_ids = owner * RES_DEV + page_table
    slot_ids = owner * (N_ROWS * CAP) + jnp.maximum(page_table - RES_DEV, 0)
    swap_ids = N_ROWS * RES_DEV + landing[slot_ids]
    page_ids = jnp.where(page_table < RES_DEV, resident_ids, swap_ids).astype(jnp.int32)
    page_store = jnp.concatenate([resident, swap_area], axis=0)
    score_scale = 1.0 / math.sqrt(HD)
    causal = jnp.arange(STEPS)[None, :] <= jnp.arange(STEPS)[:, None]

    def one_row(inputs):
        query_row, entry_row, id_row, length = inputs
        fetched = page_store[id_row]
        cached_keys = fetched[:, 0].reshape(MAXLEN, KVH, HD).astype(jnp.float32)
        cached_values = fetched[:, 1].reshape(MAXLEN, KVH, HD).astype(jnp.float32)
        head_queries = query_row.reshape(STEPS, KVH, GQ, HD).astype(jnp.float32)
        new_keys = entry_row[:, 0].reshape(STEPS, KVH, HD).astype(jnp.float32)
        new_values = entry_row[:, 1].reshape(STEPS, KVH, HD).astype(jnp.float32)
        cached_scores = jnp.einsum('skgd,lkd->kgsl', head_queries, cached_keys) * score_scale
        new_scores = jnp.einsum('skgd,tkd->kgst', head_queries, new_keys) * score_scale
        visible = jnp.arange(MAXLEN) < length
        cached_scores = jnp.where(visible[None, None, None, :], cached_scores, -1e+30)
        new_scores = jnp.where(causal[None, None], new_scores, -1e+30)
        row_peak = jnp.maximum(lax.optimization_barrier(jnp.max(cached_scores, axis=-1)), lax.optimization_barrier(jnp.max(new_scores, axis=-1)))[..., None]
        cached_exp = jnp.exp(cached_scores - row_peak)
        new_exp = jnp.exp(new_scores - row_peak)
        row_total = (lax.optimization_barrier(jnp.sum(cached_exp, axis=-1)) + lax.optimization_barrier(jnp.sum(new_exp, axis=-1)))[..., None]
        cached_weights = (cached_exp / row_total).astype(jnp.bfloat16).astype(jnp.float32)
        new_weights = (new_exp / row_total).astype(jnp.bfloat16).astype(jnp.float32)
        mixed_heads = jnp.einsum('kgsl,lkd->skgd', cached_weights, cached_values)
        mixed_heads = mixed_heads + jnp.einsum('kgst,tkd->skgd', new_weights, new_values)
        return mixed_heads.reshape(STEPS, D).astype(jnp.bfloat16)
    attended = lax.map(one_row, (queries, new_entries, page_ids, lengths))
    tokens_flat = attended.reshape(BATCH * STEPS, D)
    tokens_wide = tokens_flat.astype(jnp.float32)
    mean_square = lax.optimization_barrier(jnp.mean(tokens_wide * tokens_wide, axis=1))
    normed = (tokens_wide * norm_gain.astype(jnp.float32)[None, :]).astype(jnp.bfloat16)
    factor = lax.rsqrt(mean_square + epsilon)[:, None]
    gate = factor * jnp.dot(normed, gate_weight, preferred_element_type=jnp.float32)
    up_value = factor * jnp.dot(normed, up_weight, preferred_element_type=jnp.float32)
    hidden = (jax.nn.silu(gate) * up_value).astype(jnp.bfloat16)
    down_sum = jnp.dot(hidden, down_weight, preferred_element_type=jnp.float32)
    layer_out = (tokens_wide + down_sum).astype(jnp.bfloat16).reshape(BATCH, STEPS, D)
    return (attended, layer_out)
```

```python
import math

import jax
import jax.numpy as jnp
from jax import lax
from jax.sharding import Mesh
from jax.sharding import PartitionSpec as P

GQ = 8
HD = 128
PAGE = 16
CAP = 2

AXES = ("ylo", "x", "zhi", "zlo", "yhi", "core")
SIZES = (2, 4, 4, 4, 2, 2)
BLK = ("ylo", "x")
ROWS = ("zhi", "zlo", "yhi", "core")
FAR = ("zhi", "yhi")
SWAP = [(0, 1), (1, 0)]

epsilon = 1e-05


def spread(part, axes):
    count = lax.axis_size(axes)
    copies = jnp.broadcast_to(part[None], (count,) + part.shape)
    arrived = lax.all_to_all(copies, axes, split_axis=0, concat_axis=0, tiled=True)
    return arrived.reshape((count * part.shape[0],) + part.shape[1:])


def collect(parts, axes):
    arrived = lax.all_to_all(parts, axes, split_axis=0, concat_axis=0, tiled=True)
    return jnp.sum(arrived.astype(jnp.float32), axis=0)


def attention(queries, new_entries, resident, swap_area, swap_dest, page_table, lengths):
    owners = lax.axis_size(ROWS)
    swap_count = swap_area.shape[0]
    page_width = swap_area.shape[1] * swap_area.shape[2] * swap_area.shape[3]
    flat_swap = swap_area.reshape(swap_count, page_width)
    target = swap_dest[:, None] == jnp.arange(owners, dtype=jnp.int32)[None, :]
    before = jnp.cumsum(target.astype(jnp.int32), axis=0) - 1
    page_rank = jnp.sum(jnp.where(target, before, 0), axis=1)
    send_slot = swap_dest * CAP + page_rank
    placement = (jnp.arange(owners * CAP, dtype=jnp.int32)[:, None] == send_slot[None, :]).astype(
        jnp.bfloat16
    )
    outgoing = jnp.dot(placement, flat_swap, preferred_element_type=jnp.float32).astype(
        jnp.bfloat16
    )
    outgoing = outgoing.reshape(owners, CAP, page_width)
    arrived = lax.all_to_all(outgoing, ROWS, split_axis=0, concat_axis=0, tiled=True)
    page_store = jnp.concatenate(
        [resident.reshape(-1, page_width), arrived.reshape(owners * CAP, page_width)], axis=0
    )
    fetched = page_store[page_table]
    rows_here, pages_row = page_table.shape
    step_count = queries.shape[1]
    kv_heads = new_entries.shape[-1] // HD
    fetched = fetched.reshape(rows_here, pages_row, 2, PAGE, kv_heads, HD)
    cached_keys = fetched[:, :, 0].reshape(rows_here, pages_row * PAGE, kv_heads, HD)
    cached_values = fetched[:, :, 1].reshape(rows_here, pages_row * PAGE, kv_heads, HD)
    head_queries = queries.reshape(rows_here, step_count, kv_heads, GQ, HD)
    step_entries = new_entries.reshape(rows_here, step_count, 2, kv_heads, HD)
    score_scale = 1.0 / math.sqrt(HD)
    cached_scores = (
        jnp.einsum(
            "rskgd,rlkd->rkgsl", head_queries, cached_keys, preferred_element_type=jnp.float32
        )
        * score_scale
    )
    new_scores = (
        jnp.einsum(
            "rskgd,rtkd->rkgst",
            head_queries,
            step_entries[:, :, 0],
            preferred_element_type=jnp.float32,
        )
        * score_scale
    )
    visible = jnp.arange(pages_row * PAGE, dtype=jnp.int32)[None, :] < lengths[:, None]
    causal = jnp.arange(step_count)[None, :] <= jnp.arange(step_count)[:, None]
    cached_scores = jnp.where(visible[:, None, None, None, :], cached_scores, -1e30)
    new_scores = jnp.where(causal[None, None, None], new_scores, -1e30)
    row_peak = jnp.maximum(jnp.max(cached_scores, axis=-1), jnp.max(new_scores, axis=-1))[..., None]
    cached_exp = jnp.exp(cached_scores - row_peak)
    new_exp = jnp.exp(new_scores - row_peak)
    row_total = (jnp.sum(cached_exp, axis=-1) + jnp.sum(new_exp, axis=-1))[..., None]
    cached_weights = (cached_exp / row_total).astype(jnp.bfloat16)
    new_weights = (new_exp / row_total).astype(jnp.bfloat16)
    mixed_heads = jnp.einsum(
        "rkgsl,rlkd->rskgd", cached_weights, cached_values, preferred_element_type=jnp.float32
    )
    mixed_heads = mixed_heads + jnp.einsum(
        "rkgst,rtkd->rskgd", new_weights, step_entries[:, :, 1], preferred_element_type=jnp.float32
    )
    return mixed_heads.reshape(rows_here, step_count, -1).astype(jnp.bfloat16)


def gated_parts(tokens, norm_gain, gate_weight, up_weight):
    wide = tokens.astype(jnp.float32)
    squares = jnp.sum(wide * wide, axis=1, keepdims=True)
    squares_high = squares.astype(jnp.bfloat16)
    squares_low = (squares - squares_high.astype(jnp.float32)).astype(jnp.bfloat16)
    normed = (wide * norm_gain.astype(jnp.float32)[None, :]).astype(jnp.bfloat16)
    gate_part = jnp.dot(normed, gate_weight, preferred_element_type=jnp.float32)
    up_part = jnp.dot(normed, up_weight, preferred_element_type=jnp.float32)
    count, units = gate_part.shape
    gap = jnp.zeros((count, 512 - units - 2), jnp.bfloat16)
    tail = jnp.zeros((count, 512 - units), jnp.bfloat16)
    return jnp.concatenate(
        [
            gate_part.astype(jnp.bfloat16),
            squares_high,
            squares_low,
            gap,
            up_part.astype(jnp.bfloat16),
            tail,
        ],
        axis=1,
    )


def mlp(attended, norm_gain, gate_weight, up_weight, down_weight):
    rows_here, step_count, width = attended.shape
    local_tokens = attended.reshape(rows_here * step_count, width)
    far = lax.axis_size(FAR)
    near = lax.axis_size("zlo")
    blk = lax.axis_size(BLK)
    units = gate_weight.shape[1]
    own = spread(spread(local_tokens, FAR), "zlo")
    other = lax.ppermute(own, "core", SWAP)
    half = own.shape[0]
    parts = jnp.concatenate(
        [
            gated_parts(own, norm_gain, gate_weight, up_weight),
            gated_parts(other, norm_gain, gate_weight, up_weight),
        ],
        axis=0,
    )
    summed = collect(parts.reshape(blk, 2 * half // blk, 1024), BLK)
    gate_sum = summed[:, :units]
    up_sum = summed[:, 512 : 512 + units]
    square_sum = summed[:, units : units + 1] + summed[:, units + 1 : units + 2]
    factor = lax.rsqrt(square_sum / (width * blk) + epsilon)
    hidden = (jax.nn.silu(factor * gate_sum) * (factor * up_sum)).astype(jnp.bfloat16)
    hidden = spread(hidden, BLK)
    away = jnp.dot(hidden[half:], down_weight, preferred_element_type=jnp.float32)
    received = lax.ppermute(away.astype(jnp.bfloat16), "core", SWAP)
    kept = jnp.dot(hidden[:half], down_weight, preferred_element_type=jnp.float32)
    kept = (kept + received.astype(jnp.float32)).astype(jnp.bfloat16)
    kept = collect(kept.reshape(near, half // near, width), "zlo").astype(jnp.bfloat16)
    down_sum = collect(kept.reshape(far, half // near // far, width), FAR)
    layer_out = (local_tokens.astype(jnp.float32) + down_sum).astype(jnp.bfloat16)
    return layer_out.reshape(rows_here, step_count, width)


def on_device(
    queries,
    new_entries,
    resident,
    swap_area,
    swap_dest,
    page_table,
    lengths,
    norm_gain,
    gate_weight,
    up_weight,
    down_weight,
):
    attended = attention(
        queries, new_entries, resident, swap_area, swap_dest, page_table, lengths
    )
    return attended, mlp(attended, norm_gain, gate_weight, up_weight, down_weight)


def solution(mesh):
    fine = Mesh(mesh.devices.reshape(SIZES), AXES)
    placed = (
        P(ROWS, None, BLK),
        P(ROWS, None, None, BLK),
        P(ROWS, None, None, BLK),
        P(ROWS, None, None, BLK),
        P(ROWS),
        P(ROWS, None),
        P(ROWS),
        P(BLK),
        P(BLK, ROWS),
        P(BLK, ROWS),
        P(ROWS, BLK),
    )
    return jax.shard_map(
        on_device,
        mesh=fine,
        in_specs=placed,
        out_specs=(P(ROWS, None, BLK), P(ROWS, None, BLK)),
        check_vma=False,
    )
```

```python
import math

import jax
import jax.numpy as jnp
from jax import lax
from jax.experimental import pallas as pl
from jax.experimental.pallas import tpu as pltpu
from jax.sharding import Mesh
from jax.sharding import PartitionSpec as P

GQ = 8
HD = 128
PAGE = 16
CAP = 2

AXES = ("ylo", "x", "zhi", "zlo", "yhi", "core")
SIZES = (2, 4, 4, 4, 2, 2)
BLK = ("ylo", "x")
ROWS = ("zhi", "zlo", "yhi", "core")
NEAR = ("zlo", "yhi", "core")
MID = ("zlo", "yhi")
SWAP = [(0, 1), (1, 0)]

epsilon = 1e-05


def spread(part, axes):
    count = lax.axis_size(axes)
    copies = jnp.broadcast_to(part[None], (count,) + part.shape)
    arrived = lax.all_to_all(copies, axes, split_axis=0, concat_axis=0, tiled=True)
    return arrived.reshape((count * part.shape[0],) + part.shape[1:])


def collect(parts, axes):
    arrived = lax.all_to_all(parts, axes, split_axis=0, concat_axis=0, tiled=True)
    return jnp.sum(arrived.astype(jnp.float32), axis=0)


def stack_heads(wide):
    count = wide.shape[1] // HD
    return jnp.concatenate([wide[:, g * HD : (g + 1) * HD] for g in range(count)], axis=0)


def attend_kernel(far_ref, *refs):
    pages_ref, resident_ref, new_ref, seen_ref, out_ref = refs[-5:]
    asked_refs = refs[:-5]
    far = far_ref[0]
    owners = len(asked_refs)
    tokens, columns = asked_refs[0].shape
    width = columns - HD
    heads = width // HD
    queries = heads * tokens
    score_scale = 1.0 / math.sqrt(HD)
    token = lax.broadcasted_iota(jnp.int32, (queries, 1), 0) & (tokens - 1)
    step_count = tokens // 2
    sign = jnp.where(token < step_count, 1.0, -1.0)

    def scores(asked, keys):
        return score_scale * lax.dot_general(
            asked, keys, (((1,), (1,)), ((), ())), preferred_element_type=jnp.float32
        )

    def mix(weight, values):
        high = weight.astype(jnp.bfloat16)
        low = (weight - high.astype(jnp.float32)).astype(jnp.bfloat16)
        return jnp.dot(high, values, preferred_element_type=jnp.float32) + jnp.dot(
            low, values, preferred_element_type=jnp.float32
        )

    def page_mask(seen):
        offset = lax.broadcasted_iota(jnp.int32, seen.shape, 1) & (PAGE - 1)
        return sign * seen > offset.astype(jnp.float32)

    def heads_of(index):
        return stack_heads(asked_refs[index][:, :width].astype(jnp.float32)).astype(jnp.bfloat16)

    asked = heads_of(0)
    pages = resident_ref.shape[0]
    keys = resident_ref[:, 0].reshape(pages * PAGE, HD)
    values = resident_ref[:, 1].reshape(pages * PAGE, HD)
    mask = page_mask(seen_ref[...])
    score = jnp.where(mask, scores(asked, keys), -1e30)
    fresh = scores(asked, new_ref[0])
    other = lax.broadcasted_iota(jnp.int32, (1, fresh.shape[1]), 1)
    start = jnp.where(token < step_count, 0, step_count)
    fresh_mask = (other >= start) & (other <= token)
    fresh = jnp.where(fresh_mask, fresh, -1e30)
    own_peak = jnp.maximum(
        jnp.max(score, axis=1, keepdims=True), jnp.max(fresh, axis=1, keepdims=True)
    )
    weight = jnp.exp(score - own_peak)
    fresh_weight = jnp.exp(fresh - own_peak)
    own_total = jnp.sum(weight, axis=1, keepdims=True) + jnp.sum(
        fresh_weight, axis=1, keepdims=True
    )
    own_mixed = mix(weight, values) + mix(fresh_weight, new_ref[1])

    senders, landed = pages_ref.shape[0], pages_ref.shape[1]
    slots = landed // owners
    key_count = senders * slots * PAGE
    place = lax.broadcasted_iota(jnp.int32, (HD, key_count), 1) // PAGE + far * (senders * slots)
    expand = (lax.broadcasted_iota(jnp.int32, (HD, key_count), 0) == place).astype(jnp.float32)
    lane = lax.broadcasted_iota(jnp.int32, (tokens, HD), 1)
    for back in range(owners):
        owner = (far - back) & (owners - 1)
        table = asked_refs[back][:, width:]
        seen = jnp.dot(table, expand.astype(jnp.bfloat16), preferred_element_type=jnp.float32)[0:1]
        asked = heads_of(back)
        mine = pages_ref[:, pl.ds(owner * slots, slots)]
        keys = mine[:, :, 0].reshape(key_count, HD)
        values = mine[:, :, 1].reshape(key_count, HD)
        mask = page_mask(seen)
        score = jnp.where(mask, scores(asked, keys), -1e30)
        peak = jnp.max(score, axis=1, keepdims=True)
        weight = jnp.where(mask, jnp.exp(score - peak), 0.0)
        total = jnp.sum(weight, axis=1, keepdims=True)
        mixed = mix(weight, values)
        top = jnp.maximum(peak, own_peak) if back == 0 else peak
        top = top.astype(jnp.bfloat16).astype(jnp.float32)
        here = jnp.where(total > 0.0, jnp.exp(jnp.minimum(peak - top, 80.0)), 0.0)
        total = here * total
        mixed = here * mixed
        if back == 0:
            own = jnp.exp(jnp.minimum(own_peak - top, 80.0))
            total = total + own * own_total
            mixed = mixed + own * own_mixed
        mixed = mixed / jnp.where(total > 0.0, total, 1.0)
        total_high = total.astype(jnp.bfloat16).astype(jnp.float32)
        total_low = total - total_high
        stats = jnp.zeros((tokens, HD), jnp.float32)
        for g in range(heads):
            rows = slice(g * tokens, (g + 1) * tokens)
            stats = jnp.where(lane == g, top[rows], stats)
            stats = jnp.where(lane == heads + g, total_high[rows], stats)
            stats = jnp.where(lane == 2 * heads + g, total_low[rows], stats)
        line = jnp.concatenate(
            [mixed[g * tokens : (g + 1) * tokens] for g in range(heads)] + [stats], axis=1
        ).astype(jnp.bfloat16)
        for copy in range(out_ref.shape[0]):
            out_ref[copy, owner] = line


def merge_kernel(far_ref, parts_ref, copies_ref, attended_ref):
    sources, owners, tokens, columns = parts_ref.shape
    width = columns - HD
    heads = width // HD
    count = owners * tokens
    parts = [parts_ref[i].reshape(count, columns) for i in range(sources)]
    stats = [part[:, width:].astype(jnp.float32) for part in parts]
    peaks = [stat[:, :heads] for stat in stats]
    totals = [stat[:, heads : 2 * heads] + stat[:, 2 * heads : 3 * heads] for stat in stats]
    top = peaks[0]
    for peak in peaks[1:]:
        top = jnp.maximum(top, peak)
    shares = [total * jnp.exp(peak - top) for peak, total in zip(peaks, totals)]
    whole = shares[0]
    for share in shares[1:]:
        whole = whole + share
    shares = [share / whole for share in shares]
    blocks = []
    for g in range(heads):
        block = jnp.zeros((count, HD), jnp.float32)
        for part, share in zip(parts, shares):
            block = block + share[:, g : g + 1] * part[:, g * HD : (g + 1) * HD].astype(jnp.float32)
        blocks.append(block)
    merged = jnp.concatenate(blocks, axis=1)
    line = merged.astype(jnp.bfloat16)
    for copy in range(copies_ref.shape[0]):
        copies_ref[copy] = line
    own = merged[:tokens]
    for owner in range(1, owners):
        own = jnp.where(far_ref[0] == owner, merged[owner * tokens : (owner + 1) * tokens], own)
    attended_ref[...] = own.astype(jnp.bfloat16)


def attention(queries, new_entries, resident, swap_area, swap_dest, page_table, lengths):
    owners = lax.axis_size(ROWS)
    far_count = lax.axis_size("zhi")
    near_count = lax.axis_size(NEAR)
    mid_count = lax.axis_size(MID)
    far = lax.axis_index("zhi").astype(jnp.int32).reshape(1)
    rows_here, step_count, width = queries.shape
    tokens = rows_here * step_count
    pages_row = page_table.shape[1]
    pages_here = resident.shape[0]

    first = jnp.arange(pages_row, dtype=jnp.int32)[None, :] * PAGE
    seen = jnp.clip(lengths[:, None] - first, 0, PAGE) * jnp.array([[1], [-1]], jnp.int32)
    entries = jnp.arange(pages_here + owners * CAP, dtype=jnp.int32)
    named = page_table[:, :, None] == entries[None, None, :]
    seen = jnp.sum(jnp.where(named, seen[:, :, None], 0), axis=(0, 1)).astype(jnp.float32)
    table = jnp.pad(seen[None, pages_here:].astype(jnp.bfloat16), ((0, tokens - 1), (0, 0)))
    asked = jnp.concatenate([queries.reshape(tokens, width), table], axis=1)
    asked = [asked] + [
        lax.ppermute(asked, "zhi", [(i, (i + back) % far_count) for i in range(far_count)])
        for back in range(1, far_count)
    ]
    seen_here = jnp.repeat(seen[:pages_here], PAGE)[None, :]

    swap_count = swap_area.shape[0]
    page_width = swap_area.shape[1] * swap_area.shape[2] * swap_area.shape[3]
    same = swap_dest[:, None] == swap_dest[None, :]
    earlier = jnp.arange(swap_count)[None, :] < jnp.arange(swap_count)[:, None]
    page_rank = jnp.sum((same & earlier).astype(jnp.int32), axis=1)
    send_slot = (swap_dest % near_count) * (far_count * CAP) + (
        swap_dest // near_count
    ) * CAP + page_rank
    placement = (jnp.arange(owners * CAP, dtype=jnp.int32)[:, None] == send_slot[None, :]).astype(
        jnp.bfloat16
    )
    outgoing = jnp.dot(
        placement, swap_area.reshape(swap_count, page_width), preferred_element_type=jnp.float32
    ).astype(jnp.bfloat16)
    outgoing = outgoing.reshape((near_count, far_count * CAP) + swap_area.shape[1:])
    landed = lax.all_to_all(outgoing, NEAR, split_axis=0, concat_axis=0, tiled=True)

    fresh = new_entries.reshape(tokens, 2, HD).transpose(1, 0, 2)
    fresh = jnp.pad(fresh, ((0, 0), (0, HD - tokens), (0, 0)))
    whole = pl.BlockSpec(memory_space=pltpu.VMEM)
    scalar = pl.BlockSpec(memory_space=pltpu.SMEM)
    parts = pl.pallas_call(
        attend_kernel,
        out_shape=jax.ShapeDtypeStruct((far_count, far_count, tokens, width + HD), jnp.bfloat16),
        in_specs=[scalar] + [whole] * (far_count + 4),
        out_specs=whole,
    )(far, *asked, landed, resident, fresh, seen_here)
    parts = lax.all_to_all(parts, "zhi", split_axis=0, concat_axis=0, tiled=True)
    copies, attended = pl.pallas_call(
        merge_kernel,
        out_shape=(
            jax.ShapeDtypeStruct((mid_count, far_count * tokens, width), jnp.bfloat16),
            jax.ShapeDtypeStruct((tokens, width), jnp.bfloat16),
        ),
        in_specs=[scalar, whole],
        out_specs=(whole, whole),
    )(far, parts)
    return copies, attended


def gated_parts(tokens, norm_gain, gate_weight, up_weight):
    wide = tokens.astype(jnp.float32)
    squares = jnp.sum(wide * wide, axis=1, keepdims=True)
    squares_high = squares.astype(jnp.bfloat16)
    squares_low = (squares - squares_high.astype(jnp.float32)).astype(jnp.bfloat16)
    normed = (wide * norm_gain.astype(jnp.float32)[None, :]).astype(jnp.bfloat16)
    gate_part = jnp.dot(normed, gate_weight, preferred_element_type=jnp.float32)
    up_part = jnp.dot(normed, up_weight, preferred_element_type=jnp.float32)
    count, units = gate_part.shape
    gap = jnp.zeros((count, 512 - units - 2), jnp.bfloat16)
    tail = jnp.zeros((count, 512 - units), jnp.bfloat16)
    return jnp.concatenate(
        [
            gate_part.astype(jnp.bfloat16),
            squares_high,
            squares_low,
            gap,
            up_part.astype(jnp.bfloat16),
            tail,
        ],
        axis=1,
    )


def mlp(copies, attended, norm_gain, gate_weight, up_weight, down_weight):
    tokens_here, width = attended.shape
    far = lax.axis_size("zhi")
    mid = lax.axis_size(MID)
    blk = lax.axis_size(BLK)
    units = gate_weight.shape[1]
    own = lax.all_to_all(copies, MID, split_axis=0, concat_axis=0, tiled=True).reshape(-1, width)
    other = lax.ppermute(own, "core", SWAP)
    half = own.shape[0]
    parts = jnp.concatenate(
        [
            gated_parts(own, norm_gain, gate_weight, up_weight),
            gated_parts(other, norm_gain, gate_weight, up_weight),
        ],
        axis=0,
    )
    summed = collect(parts.reshape(blk, 2 * half // blk, 1024), BLK)
    gate_sum = summed[:, :units]
    up_sum = summed[:, 512 : 512 + units]
    square_sum = summed[:, units : units + 1] + summed[:, units + 1 : units + 2]
    factor = lax.rsqrt(square_sum / (width * blk) + epsilon)
    hidden = (jax.nn.silu(factor * gate_sum) * (factor * up_sum)).astype(jnp.bfloat16)
    hidden = spread(hidden, BLK)
    away = jnp.dot(hidden[half:], down_weight, preferred_element_type=jnp.float32)
    received = lax.ppermute(away.astype(jnp.bfloat16), "core", SWAP)
    kept = jnp.dot(hidden[:half], down_weight, preferred_element_type=jnp.float32)
    kept = (kept + received.astype(jnp.float32)).astype(jnp.bfloat16)
    kept = collect(kept.reshape(mid, far * tokens_here, width), MID).astype(jnp.bfloat16)
    down_sum = collect(kept.reshape(far, tokens_here, width), "zhi")
    return (attended.astype(jnp.float32) + down_sum).astype(jnp.bfloat16)


def on_device(
    queries,
    new_entries,
    resident,
    swap_area,
    swap_dest,
    page_table,
    lengths,
    norm_gain,
    gate_weight,
    up_weight,
    down_weight,
):
    copies, attended = attention(
        queries, new_entries, resident, swap_area, swap_dest, page_table, lengths
    )
    layer_out = mlp(copies, attended, norm_gain, gate_weight, up_weight, down_weight)
    return attended.reshape(queries.shape), layer_out.reshape(queries.shape)


def solution(mesh):
    fine = Mesh(mesh.devices.reshape(SIZES), AXES)
    placed = (
        P(ROWS, None, BLK),
        P(ROWS, None, None, BLK),
        P(ROWS, None, None, BLK),
        P(ROWS, None, None, BLK),
        P(ROWS),
        P(ROWS, None),
        P(ROWS),
        P(BLK),
        P(BLK, ROWS),
        P(BLK, ROWS),
        P(ROWS, BLK),
    )
    return jax.shard_map(
        on_device,
        mesh=fine,
        in_specs=placed,
        out_specs=(P(ROWS, None, BLK), P(ROWS, None, BLK)),
        check_vma=False,
    )
```

```python
import math

import jax
import jax.numpy as jnp
from jax import lax
from jax.experimental import pallas as pl
from jax.experimental.pallas import tpu as pltpu
from jax.sharding import Mesh
from jax.sharding import PartitionSpec as P

GQ = 8
HD = 128
PAGE = 16
CAP = 2

AXES = ("ylo", "x", "zhi", "zlo", "yhi", "core")
SIZES = (2, 4, 4, 4, 2, 2)
BLK = ("ylo", "x")
ROWS = ("zhi", "zlo", "yhi", "core")
NEAR = ("zlo", "yhi", "core")
MID = ("zlo", "yhi")
SWAP = [(0, 1), (1, 0)]

epsilon = 1e-05


def spread(part, axes):
    count = lax.axis_size(axes)
    copies = jnp.broadcast_to(part[None], (count,) + part.shape)
    arrived = lax.all_to_all(copies, axes, split_axis=0, concat_axis=0, tiled=True)
    return arrived.reshape((count * part.shape[0],) + part.shape[1:])


def collect(parts, axes):
    arrived = lax.all_to_all(parts, axes, split_axis=0, concat_axis=0, tiled=True)
    return jnp.sum(arrived.astype(jnp.float32), axis=0)


def stack_heads(wide):
    count = wide.shape[1] // HD
    return jnp.concatenate([wide[:, g * HD : (g + 1) * HD] for g in range(count)], axis=0)


def head_rows(wide):
    return stack_heads(wide.astype(jnp.float32)).astype(jnp.bfloat16)


def scores(asked, keys):
    return (1.0 / math.sqrt(HD)) * lax.dot_general(
        asked, keys, (((1,), (1,)), ((), ())), preferred_element_type=jnp.float32
    )


def mix(weight, values):
    high = weight.astype(jnp.bfloat16)
    low = (weight - high.astype(jnp.float32)).astype(jnp.bfloat16)
    return jnp.dot(high, values, preferred_element_type=jnp.float32) + jnp.dot(
        low, values, preferred_element_type=jnp.float32
    )


def page_mask(token, step_count, seen):
    sign = jnp.where(token < step_count, 1.0, -1.0)
    offset = lax.broadcasted_iota(jnp.int32, seen.shape, 1) & (PAGE - 1)
    return sign * seen > offset.astype(jnp.float32)


def resident_kernel(asked_ref, resident_ref, new_ref, seen_ref, mixed_ref, peak_ref, total_ref):
    tokens, columns = asked_ref.shape
    width = columns - HD
    step_count = tokens // 2
    queries = width // HD * tokens
    token = lax.broadcasted_iota(jnp.int32, (queries, 1), 0) & (tokens - 1)
    asked = head_rows(asked_ref[:, :width])
    pages = resident_ref.shape[0]
    keys = resident_ref[:, 0].reshape(pages * PAGE, HD)
    values = resident_ref[:, 1].reshape(pages * PAGE, HD)
    mask = page_mask(token, step_count, seen_ref[...])
    score = jnp.where(mask, scores(asked, keys), -1e30)
    fresh = scores(asked, new_ref[0])
    other = lax.broadcasted_iota(jnp.int32, (1, fresh.shape[1]), 1)
    start = jnp.where(token < step_count, 0, step_count)
    fresh = jnp.where((other >= start) & (other <= token), fresh, -1e30)
    peak = jnp.maximum(
        jnp.max(score, axis=1, keepdims=True), jnp.max(fresh, axis=1, keepdims=True)
    )
    weight = jnp.exp(score - peak)
    fresh_weight = jnp.exp(fresh - peak)
    total = jnp.sum(weight, axis=1, keepdims=True) + jnp.sum(fresh_weight, axis=1, keepdims=True)
    mixed_ref[...] = mix(weight, values) + mix(fresh_weight, new_ref[1])
    peak_ref[...] = jnp.broadcast_to(peak, peak_ref.shape)
    total_ref[...] = jnp.broadcast_to(total, total_ref.shape)


def attend_kernel(far_ref, *refs):
    far = far_ref[0]
    pages_ref, mixed_ref, peak_ref, total_ref, out_ref = refs[-5:]
    asked_of = [ref[...] for ref in refs[:-5]]
    owners = len(asked_of)
    tokens, columns = asked_of[0].shape
    width = columns - HD
    heads = width // HD
    queries = heads * tokens
    token = lax.broadcasted_iota(jnp.int32, (queries, 1), 0) & (tokens - 1)
    senders, landed = pages_ref.shape[0], pages_ref.shape[1]
    slots = landed // owners
    key_count = senders * slots * PAGE
    place = lax.broadcasted_iota(jnp.int32, (HD, key_count), 1) // PAGE + far * (senders * slots)
    expand = (lax.broadcasted_iota(jnp.int32, (HD, key_count), 0) == place).astype(jnp.float32)
    expand = expand.astype(jnp.bfloat16)
    lane = lax.broadcasted_iota(jnp.int32, (tokens, HD), 1)
    for flip in range(owners):
        owner = far ^ flip
        table = asked_of[flip][:, width:]
        seen = jnp.dot(table, expand, preferred_element_type=jnp.float32)[0:1]
        asked = head_rows(asked_of[flip][:, :width])
        mine = pages_ref[:, pl.ds(owner * slots, slots)]
        keys = mine[:, :, 0].reshape(key_count, HD)
        values = mine[:, :, 1].reshape(key_count, HD)
        mask = page_mask(token, tokens // 2, seen)
        score = jnp.where(mask, scores(asked, keys), -1e30)
        peak = jnp.max(score, axis=1, keepdims=True)
        weight = jnp.where(mask, jnp.exp(score - peak), 0.0)
        total = jnp.sum(weight, axis=1, keepdims=True)
        mixed = mix(weight, values)
        own_peak = peak_ref[:, :1]
        top = jnp.maximum(peak, own_peak) if flip == 0 else peak
        top = top.astype(jnp.bfloat16).astype(jnp.float32)
        here = jnp.where(total > 0.0, jnp.exp(jnp.minimum(peak - top, 80.0)), 0.0)
        total = here * total
        mixed = here * mixed
        if flip == 0:
            own = jnp.exp(jnp.minimum(own_peak - top, 80.0))
            total = total + own * total_ref[:, :1]
            mixed = mixed + own * mixed_ref[...]
        mixed = mixed / jnp.where(total > 0.0, total, 1.0)
        total_high = total.astype(jnp.bfloat16).astype(jnp.float32)
        total_low = total - total_high
        stats = jnp.zeros((tokens, HD), jnp.float32)
        for g in range(heads):
            rows = slice(g * tokens, (g + 1) * tokens)
            stats = jnp.where(lane == g, top[rows], stats)
            stats = jnp.where(lane == heads + g, total_high[rows], stats)
            stats = jnp.where(lane == 2 * heads + g, total_low[rows], stats)
        line = jnp.concatenate(
            [mixed[g * tokens : (g + 1) * tokens] for g in range(heads)] + [stats], axis=1
        ).astype(jnp.bfloat16)
        for copy in range(out_ref.shape[0]):
            out_ref[copy, owner] = line


def merge_kernel(far_ref, parts_ref, copies_ref, attended_ref):
    sources, owners, tokens, columns = parts_ref.shape
    width = columns - HD
    heads = width // HD
    count = owners * tokens
    parts = [parts_ref[i].reshape(count, columns) for i in range(sources)]
    stats = [part[:, width:].astype(jnp.float32) for part in parts]
    peaks = [stat[:, :heads] for stat in stats]
    totals = [stat[:, heads : 2 * heads] + stat[:, 2 * heads : 3 * heads] for stat in stats]
    top = peaks[0]
    for peak in peaks[1:]:
        top = jnp.maximum(top, peak)
    shares = [total * jnp.exp(peak - top) for peak, total in zip(peaks, totals)]
    whole = shares[0]
    for share in shares[1:]:
        whole = whole + share
    shares = [share / whole for share in shares]
    blocks = []
    for g in range(heads):
        block = jnp.zeros((count, HD), jnp.float32)
        for part, share in zip(parts, shares):
            block = block + share[:, g : g + 1] * part[:, g * HD : (g + 1) * HD].astype(jnp.float32)
        blocks.append(block)
    merged = jnp.concatenate(blocks, axis=1)
    line = merged.astype(jnp.bfloat16)
    for copy in range(copies_ref.shape[0]):
        copies_ref[copy] = line
    own = merged[:tokens]
    for owner in range(1, owners):
        own = jnp.where(far_ref[0] == owner, merged[owner * tokens : (owner + 1) * tokens], own)
    attended_ref[...] = own.astype(jnp.bfloat16)


def attention(
    queries, new_entries, resident, swap_area, swap_dest, page_table, lengths, weights
):
    owners = lax.axis_size(ROWS)
    far_count = lax.axis_size("zhi")
    near_count = lax.axis_size(NEAR)
    mid_count = lax.axis_size(MID)
    far = lax.axis_index("zhi").astype(jnp.int32).reshape(1)
    rows_here, step_count, width = queries.shape
    tokens = rows_here * step_count
    pages_row = page_table.shape[1]
    pages_here = resident.shape[0]

    first = jnp.arange(pages_row, dtype=jnp.int32)[None, :] * PAGE
    seen = jnp.clip(lengths[:, None] - first, 0, PAGE) * jnp.array([[1], [-1]], jnp.int32)
    entries = jnp.arange(pages_here + owners * CAP, dtype=jnp.int32)
    named = page_table[:, :, None] == entries[None, None, :]
    seen = jnp.sum(jnp.where(named, seen[:, :, None], 0), axis=(0, 1)).astype(jnp.float32)
    table = jnp.pad(seen[None, pages_here:].astype(jnp.bfloat16), ((0, tokens - 1), (0, 0)))
    asked = jnp.concatenate([queries.reshape(tokens, width), table], axis=1)
    asked = [asked] + [
        lax.ppermute(asked, "zhi", [(i, i ^ flip) for i in range(far_count)])
        for flip in range(1, far_count)
    ]
    seen_here = jnp.repeat(seen[:pages_here], PAGE)[None, :]

    swap_count = swap_area.shape[0]
    page_width = swap_area.shape[1] * swap_area.shape[2] * swap_area.shape[3]
    same = swap_dest[:, None] == swap_dest[None, :]
    earlier = jnp.arange(swap_count)[None, :] < jnp.arange(swap_count)[:, None]
    page_rank = jnp.sum((same & earlier).astype(jnp.int32), axis=1)
    send_slot = (swap_dest % near_count) * (far_count * CAP) + (
        swap_dest // near_count
    ) * CAP + page_rank
    placement = (jnp.arange(owners * CAP, dtype=jnp.int32)[:, None] == send_slot[None, :]).astype(
        jnp.bfloat16
    )
    outgoing = jnp.dot(
        placement, swap_area.reshape(swap_count, page_width), preferred_element_type=jnp.float32
    ).astype(jnp.bfloat16)
    outgoing = outgoing.reshape((near_count, far_count * CAP) + swap_area.shape[1:])
    landed = lax.all_to_all(outgoing, NEAR, split_axis=0, concat_axis=0, tiled=True)

    fresh = new_entries.reshape(tokens, 2, HD).transpose(1, 0, 2)
    fresh = jnp.pad(fresh, ((0, 0), (0, HD - tokens), (0, 0)))
    whole = pl.BlockSpec(memory_space=pltpu.VMEM)
    scalar = pl.BlockSpec(memory_space=pltpu.SMEM)
    queries_here = width // HD * tokens
    square = jax.ShapeDtypeStruct((queries_here, HD), jnp.float32)
    found = pl.pallas_call(
        resident_kernel,
        out_shape=(square, square, square),
        in_specs=[whole] * 4,
        out_specs=(whole, whole, whole),
        cost_estimate=pl.CostEstimate(
            flops=6 * queries_here * HD * pages_here * PAGE,
            bytes_accessed=2 * resident.size,
            transcendentals=queries_here * pages_here * PAGE,
        ),
    )(asked[0], resident, fresh, seen_here)
    parts = pl.pallas_call(
        attend_kernel,
        out_shape=jax.ShapeDtypeStruct((far_count, far_count, tokens, width + HD), jnp.bfloat16),
        in_specs=[scalar] + [whole] * (far_count + 4),
        out_specs=whole,
    )(far, *asked, landed, *found)
    parts, weights = lax.optimization_barrier((parts, weights))
    parts = lax.all_to_all(parts, "zhi", split_axis=0, concat_axis=0, tiled=True)
    copies, attended = pl.pallas_call(
        merge_kernel,
        out_shape=(
            jax.ShapeDtypeStruct((mid_count, far_count * tokens, width), jnp.bfloat16),
            jax.ShapeDtypeStruct((tokens, width), jnp.bfloat16),
        ),
        in_specs=[scalar, whole],
        out_specs=(whole, whole),
    )(far, parts)
    return copies, attended, weights


def join_weights(gate_weight, up_weight):
    units = gate_weight.shape[1]
    gap = jnp.zeros((gate_weight.shape[0], 512 - units), gate_weight.dtype)
    return jnp.concatenate([gate_weight, gap, up_weight, gap], axis=1)


def gated_parts(tokens, norm_gain, weights, units):
    wide = tokens.astype(jnp.float32)
    squares = jnp.sum(wide * wide, axis=1, keepdims=True)
    squares_high = squares.astype(jnp.bfloat16).astype(jnp.float32)
    normed = (wide * norm_gain.astype(jnp.float32)[None, :]).astype(jnp.bfloat16)
    both = jnp.dot(normed, weights, preferred_element_type=jnp.float32)
    column = jnp.arange(both.shape[1], dtype=jnp.int32)[None, :]
    both = jnp.where(column == units, squares_high, both)
    both = jnp.where(column == units + 1, squares - squares_high, both)
    return both.astype(jnp.bfloat16)


def mlp(copies, attended, norm_gain, weights, units, down_weight):
    tokens_here, width = attended.shape
    far = lax.axis_size("zhi")
    mid = lax.axis_size(MID)
    blk = lax.axis_size(BLK)
    own = lax.all_to_all(copies, MID, split_axis=0, concat_axis=0, tiled=True).reshape(-1, width)
    other = lax.ppermute(own, "core", SWAP)
    half = own.shape[0]
    parts = jnp.concatenate(
        [
            gated_parts(own, norm_gain, weights, units),
            gated_parts(other, norm_gain, weights, units),
        ],
        axis=0,
    )
    summed = collect(parts.reshape(blk, 2 * half // blk, 1024), BLK)
    gate_sum = summed[:, :units]
    up_sum = summed[:, 512 : 512 + units]
    square_sum = summed[:, units : units + 1] + summed[:, units + 1 : units + 2]
    factor = lax.rsqrt(square_sum / (width * blk) + epsilon)
    hidden = (jax.nn.silu(factor * gate_sum) * (factor * up_sum)).astype(jnp.bfloat16)
    hidden = spread(hidden, BLK)
    away = jnp.dot(hidden[half:], down_weight, preferred_element_type=jnp.float32)
    received = lax.ppermute(away.astype(jnp.bfloat16), "core", SWAP)
    kept = jnp.dot(hidden[:half], down_weight, preferred_element_type=jnp.float32)
    kept = (kept + received.astype(jnp.float32)).astype(jnp.bfloat16)
    kept = collect(kept.reshape(mid, far * tokens_here, width), MID).astype(jnp.bfloat16)
    down_sum = collect(kept.reshape(far, tokens_here, width), "zhi")
    return (attended.astype(jnp.float32) + down_sum).astype(jnp.bfloat16)


def on_device(
    queries,
    new_entries,
    resident,
    swap_area,
    swap_dest,
    page_table,
    lengths,
    norm_gain,
    gate_weight,
    up_weight,
    down_weight,
):
    weights = join_weights(gate_weight, up_weight)
    copies, attended, weights = attention(
        queries, new_entries, resident, swap_area, swap_dest, page_table, lengths, weights
    )
    units = gate_weight.shape[1]
    layer_out = mlp(copies, attended, norm_gain, weights, units, down_weight)
    return attended.reshape(queries.shape), layer_out.reshape(queries.shape)


def solution(mesh):
    fine = Mesh(mesh.devices.reshape(SIZES), AXES)
    placed = (
        P(ROWS, None, BLK),
        P(ROWS, None, None, BLK),
        P(ROWS, None, None, BLK),
        P(ROWS, None, None, BLK),
        P(ROWS),
        P(ROWS, None),
        P(ROWS),
        P(BLK),
        P(BLK, ROWS),
        P(BLK, ROWS),
        P(ROWS, BLK),
    )
    return jax.shard_map(
        on_device,
        mesh=fine,
        in_specs=placed,
        out_specs=(P(ROWS, None, BLK), P(ROWS, None, BLK)),
        check_vma=False,
    )
```

```python
import math

import jax
import jax.numpy as jnp
from jax import lax
from jax.experimental import pallas as pl
from jax.experimental.pallas import tpu as pltpu
from jax.sharding import Mesh
from jax.sharding import PartitionSpec as P

GQ = 8
HD = 128
PAGE = 16
CAP = 2

AXES = ("ylo", "x", "zhi", "zlo", "yhi", "core")
SIZES = (2, 4, 4, 4, 2, 2)
BLK = ("ylo", "x")
ROWS = ("zhi", "zlo", "yhi", "core")
NEAR = ("zlo", "yhi", "core")
MID = ("zlo", "yhi")
SWAP = [(0, 1), (1, 0)]

epsilon = 1e-05


def spread(part, axes):
    count = lax.axis_size(axes)
    copies = jnp.broadcast_to(part[None], (count,) + part.shape)
    arrived = lax.all_to_all(copies, axes, split_axis=0, concat_axis=0, tiled=True)
    return arrived.reshape((count * part.shape[0],) + part.shape[1:])


def collect(parts, axes):
    arrived = lax.all_to_all(parts, axes, split_axis=0, concat_axis=0, tiled=True)
    return jnp.sum(arrived.astype(jnp.float32), axis=0)


def stack_heads(wide):
    count = wide.shape[1] // HD
    return jnp.concatenate([wide[:, g * HD : (g + 1) * HD] for g in range(count)], axis=0)


def head_rows(wide):
    return stack_heads(wide.astype(jnp.float32)).astype(jnp.bfloat16)


def scores(asked, keys):
    return (1.0 / math.sqrt(HD)) * lax.dot_general(
        asked, keys, (((1,), (1,)), ((), ())), preferred_element_type=jnp.float32
    )


def mix(weight, values):
    high = weight.astype(jnp.bfloat16)
    low = (weight - high.astype(jnp.float32)).astype(jnp.bfloat16)
    return jnp.dot(high, values, preferred_element_type=jnp.float32) + jnp.dot(
        low, values, preferred_element_type=jnp.float32
    )


def page_mask(token, step_count, seen):
    sign = jnp.where(token < step_count, 1.0, -1.0)
    offset = lax.broadcasted_iota(jnp.int32, seen.shape, 1) & (PAGE - 1)
    return sign * seen > offset.astype(jnp.float32)


def resident_kernel(asked_ref, resident_ref, new_ref, seen_ref, mixed_ref, peak_ref, total_ref):
    tokens, columns = asked_ref.shape
    width = columns - HD
    step_count = tokens // 2
    queries = width // HD * tokens
    token = lax.broadcasted_iota(jnp.int32, (queries, 1), 0) & (tokens - 1)
    asked = head_rows(asked_ref[:, :width])
    pages = resident_ref.shape[0]
    keys = resident_ref[:, 0].reshape(pages * PAGE, HD)
    values = resident_ref[:, 1].reshape(pages * PAGE, HD)
    mask = page_mask(token, step_count, seen_ref[...])
    score = jnp.where(mask, scores(asked, keys), -1e30)
    fresh = scores(asked, new_ref[0])
    other = lax.broadcasted_iota(jnp.int32, (1, fresh.shape[1]), 1)
    start = jnp.where(token < step_count, 0, step_count)
    fresh = jnp.where((other >= start) & (other <= token), fresh, -1e30)
    peak = jnp.maximum(
        jnp.max(score, axis=1, keepdims=True), jnp.max(fresh, axis=1, keepdims=True)
    )
    weight = jnp.exp(score - peak)
    fresh_weight = jnp.exp(fresh - peak)
    total = jnp.sum(weight, axis=1, keepdims=True) + jnp.sum(fresh_weight, axis=1, keepdims=True)
    mixed_ref[...] = mix(weight, values) + mix(fresh_weight, new_ref[1])
    peak_ref[...] = jnp.broadcast_to(peak, peak_ref.shape)
    total_ref[...] = jnp.broadcast_to(total, total_ref.shape)


def attend_kernel(far_ref, *refs):
    far = far_ref[0]
    pages_ref, mixed_ref, peak_ref, total_ref, out_ref = refs[-5:]
    asked_of = [ref[...] for ref in refs[:-5]]
    owners = len(asked_of)
    tokens, columns = asked_of[0].shape
    width = columns - HD
    heads = width // HD
    queries = heads * tokens
    token = lax.broadcasted_iota(jnp.int32, (queries, 1), 0) & (tokens - 1)
    senders, landed = pages_ref.shape[0], pages_ref.shape[1]
    slots = landed // owners
    key_count = senders * slots * PAGE
    place = lax.broadcasted_iota(jnp.int32, (HD, key_count), 1) // PAGE + far * (senders * slots)
    expand = (lax.broadcasted_iota(jnp.int32, (HD, key_count), 0) == place).astype(jnp.float32)
    expand = expand.astype(jnp.bfloat16)
    lane = lax.broadcasted_iota(jnp.int32, (tokens, HD), 1)
    for flip in range(owners):
        owner = far ^ flip
        table = asked_of[flip][:, width:]
        seen = jnp.dot(table, expand, preferred_element_type=jnp.float32)[0:1]
        asked = head_rows(asked_of[flip][:, :width])
        mine = pages_ref[:, pl.ds(owner * slots, slots)]
        keys = mine[:, :, 0].reshape(key_count, HD)
        values = mine[:, :, 1].reshape(key_count, HD)
        mask = page_mask(token, tokens // 2, seen)
        score = jnp.where(mask, scores(asked, keys), -1e30)
        peak = jnp.max(score, axis=1, keepdims=True)
        weight = jnp.where(mask, jnp.exp(score - peak), 0.0)
        total = jnp.sum(weight, axis=1, keepdims=True)
        mixed = mix(weight, values)
        own_peak = peak_ref[:, :1]
        top = jnp.maximum(peak, own_peak) if flip == 0 else peak
        top = top.astype(jnp.bfloat16).astype(jnp.float32)
        here = jnp.where(total > 0.0, jnp.exp(jnp.minimum(peak - top, 80.0)), 0.0)
        total = here * total
        mixed = here * mixed
        if flip == 0:
            own = jnp.exp(jnp.minimum(own_peak - top, 80.0))
            total = total + own * total_ref[:, :1]
            mixed = mixed + own * mixed_ref[...]
        mixed = mixed / jnp.where(total > 0.0, total, 1.0)
        total_high = total.astype(jnp.bfloat16).astype(jnp.float32)
        total_low = total - total_high
        stats = jnp.zeros((tokens, HD), jnp.float32)
        for g in range(heads):
            rows = slice(g * tokens, (g + 1) * tokens)
            stats = jnp.where(lane == g, top[rows], stats)
            stats = jnp.where(lane == heads + g, total_high[rows], stats)
            stats = jnp.where(lane == 2 * heads + g, total_low[rows], stats)
        line = jnp.concatenate(
            [mixed[g * tokens : (g + 1) * tokens] for g in range(heads)] + [stats], axis=1
        ).astype(jnp.bfloat16)
        for copy in range(out_ref.shape[0]):
            out_ref[copy, owner] = line


def merge_kernel(far_ref, parts_ref, copies_ref, attended_ref):
    sources, owners, tokens, columns = parts_ref.shape
    width = columns - HD
    heads = width // HD
    count = owners * tokens
    parts = [parts_ref[i].reshape(count, columns) for i in range(sources)]
    stats = [part[:, width:].astype(jnp.float32) for part in parts]
    peaks = [stat[:, :heads] for stat in stats]
    totals = [stat[:, heads : 2 * heads] + stat[:, 2 * heads : 3 * heads] for stat in stats]
    top = peaks[0]
    for peak in peaks[1:]:
        top = jnp.maximum(top, peak)
    shares = [total * jnp.exp(peak - top) for peak, total in zip(peaks, totals)]
    whole = shares[0]
    for share in shares[1:]:
        whole = whole + share
    shares = [share / whole for share in shares]
    blocks = []
    for g in range(heads):
        block = jnp.zeros((count, HD), jnp.float32)
        for part, share in zip(parts, shares):
            block = block + share[:, g : g + 1] * part[:, g * HD : (g + 1) * HD].astype(jnp.float32)
        blocks.append(block)
    merged = jnp.concatenate(blocks, axis=1)
    line = merged.astype(jnp.bfloat16)
    for copy in range(copies_ref.shape[0]):
        copies_ref[copy] = line
    own = merged[:tokens]
    for owner in range(1, owners):
        own = jnp.where(far_ref[0] == owner, merged[owner * tokens : (owner + 1) * tokens], own)
    attended_ref[...] = own.astype(jnp.bfloat16)


def attention(
    queries, new_entries, resident, swap_area, swap_dest, page_table, lengths, weights
):
    owners = lax.axis_size(ROWS)
    far_count = lax.axis_size("zhi")
    near_count = lax.axis_size(NEAR)
    mid_count = lax.axis_size(MID)
    far = lax.axis_index("zhi").astype(jnp.int32).reshape(1)
    rows_here, step_count, width = queries.shape
    tokens = rows_here * step_count
    pages_row = page_table.shape[1]
    pages_here = resident.shape[0]

    first = jnp.arange(pages_row, dtype=jnp.int32)[None, :] * PAGE
    seen = jnp.clip(lengths[:, None] - first, 0, PAGE) * jnp.array([[1], [-1]], jnp.int32)
    entries = jnp.arange(pages_here + owners * CAP, dtype=jnp.int32)
    named = page_table[:, :, None] == entries[None, None, :]
    seen = jnp.sum(jnp.where(named, seen[:, :, None], 0), axis=(0, 1)).astype(jnp.float32)
    table = jnp.pad(seen[None, pages_here:].astype(jnp.bfloat16), ((0, tokens - 1), (0, 0)))
    asked = jnp.concatenate([queries.reshape(tokens, width), table], axis=1)
    asked = [asked] + [
        lax.ppermute(asked, "zhi", [(i, i ^ flip) for i in range(far_count)])
        for flip in range(1, far_count)
    ]
    seen_here = jnp.repeat(seen[:pages_here], PAGE)[None, :]

    swap_count = swap_area.shape[0]
    page_width = swap_area.shape[1] * swap_area.shape[2] * swap_area.shape[3]
    same = swap_dest[:, None] == swap_dest[None, :]
    earlier = jnp.arange(swap_count)[None, :] < jnp.arange(swap_count)[:, None]
    page_rank = jnp.sum((same & earlier).astype(jnp.int32), axis=1)
    send_slot = (swap_dest % near_count) * (far_count * CAP) + (
        swap_dest // near_count
    ) * CAP + page_rank
    placement = (jnp.arange(owners * CAP, dtype=jnp.int32)[:, None] == send_slot[None, :]).astype(
        jnp.bfloat16
    )
    outgoing = jnp.dot(
        placement, swap_area.reshape(swap_count, page_width), preferred_element_type=jnp.float32
    ).astype(jnp.bfloat16)
    outgoing = outgoing.reshape((near_count, far_count * CAP) + swap_area.shape[1:])
    landed = lax.all_to_all(outgoing, NEAR, split_axis=0, concat_axis=0, tiled=True)

    fresh = new_entries.reshape(tokens, 2, HD).transpose(1, 0, 2)
    fresh = jnp.pad(fresh, ((0, 0), (0, HD - tokens), (0, 0)))
    whole = pl.BlockSpec(memory_space=pltpu.VMEM)
    scalar = pl.BlockSpec(memory_space=pltpu.SMEM)
    queries_here = width // HD * tokens
    square = jax.ShapeDtypeStruct((queries_here, HD), jnp.float32)
    found = pl.pallas_call(
        resident_kernel,
        out_shape=(square, square, square),
        in_specs=[whole] * 4,
        out_specs=(whole, whole, whole),
        cost_estimate=pl.CostEstimate(
            flops=6 * queries_here * HD * pages_here * PAGE,
            bytes_accessed=2 * resident.size,
            transcendentals=queries_here * pages_here * PAGE,
        ),
    )(asked[0], resident, fresh, seen_here)
    found, weights = lax.optimization_barrier((found, weights))
    weights = join_weights(*weights)
    parts = pl.pallas_call(
        attend_kernel,
        out_shape=jax.ShapeDtypeStruct((far_count, far_count, tokens, width + HD), jnp.bfloat16),
        in_specs=[scalar] + [whole] * (far_count + 4),
        out_specs=whole,
    )(far, *asked, landed, *found)
    parts = lax.all_to_all(parts, "zhi", split_axis=0, concat_axis=0, tiled=True)
    parts, weights = lax.optimization_barrier((parts, weights))
    copies, attended = pl.pallas_call(
        merge_kernel,
        out_shape=(
            jax.ShapeDtypeStruct((mid_count, far_count * tokens, width), jnp.bfloat16),
            jax.ShapeDtypeStruct((tokens, width), jnp.bfloat16),
        ),
        in_specs=[scalar, whole],
        out_specs=(whole, whole),
    )(far, parts)
    return copies, attended, weights


def join_weights(gate_weight, up_weight, down_weight):
    units, width = down_weight.shape
    gate, up = gate_weight.T, up_weight.T
    there = lax.ppermute(jnp.concatenate([gate, up, down_weight], axis=0), "core", SWAP)
    gap = jnp.zeros((128, width), gate_weight.dtype)
    wide = jnp.concatenate([gate, there[:units], up, there[units : 2 * units], gap], axis=0)
    return wide, jnp.concatenate([down_weight, there[2 * units :]], axis=0)


def gated_parts(tokens, norm_gain, weights, units):
    wide = tokens.astype(jnp.float32)
    squares = jnp.sum(wide * wide, axis=1, keepdims=True)
    squares_high = squares.astype(jnp.bfloat16).astype(jnp.float32)
    normed = (wide * norm_gain.astype(jnp.float32)[None, :]).astype(jnp.bfloat16)
    both = lax.dot_general(
        normed, weights, (((1,), (1,)), ((), ())), preferred_element_type=jnp.float32
    )
    column = jnp.arange(both.shape[1], dtype=jnp.int32)[None, :]
    both = jnp.where(column == 2 * units, squares_high, both)
    both = jnp.where(column == 2 * units + 1, squares - squares_high, both)
    return both.astype(jnp.bfloat16)


def mlp(copies, attended, norm_gain, weights, units):
    wide_weight, down_weight = weights
    tokens_here, width = attended.shape
    far = lax.axis_size("zhi")
    mid = lax.axis_size(MID)
    blk = lax.axis_size(BLK)
    own = lax.all_to_all(copies, MID, split_axis=0, concat_axis=0, tiled=True).reshape(-1, width)
    parts = gated_parts(own, norm_gain, wide_weight, units)
    summed = collect(parts.reshape(blk, own.shape[0] // blk, parts.shape[1]), BLK)
    square_sum = summed[:, 2 * units : 2 * units + 1] + summed[:, 2 * units + 1 : 2 * units + 2]
    factor = lax.rsqrt(square_sum / (width * blk) + epsilon)
    gate_sum = summed[:, :units]
    up_sum = summed[:, units : 2 * units]
    hidden = (jax.nn.silu(factor * gate_sum) * (factor * up_sum)).astype(jnp.bfloat16)
    hidden = spread(hidden, BLK)
    kept = jnp.dot(hidden, down_weight, preferred_element_type=jnp.float32).astype(jnp.bfloat16)
    kept = collect(kept.reshape(mid, far * tokens_here, width), MID).astype(jnp.bfloat16)
    down_sum = collect(kept.reshape(far, tokens_here, width), "zhi")
    return (attended.astype(jnp.float32) + down_sum).astype(jnp.bfloat16)


def on_device(
    queries,
    new_entries,
    resident,
    swap_area,
    swap_dest,
    page_table,
    lengths,
    norm_gain,
    gate_weight,
    up_weight,
    down_weight,
):
    weights = (gate_weight, up_weight, down_weight)
    copies, attended, weights = attention(
        queries, new_entries, resident, swap_area, swap_dest, page_table, lengths, weights
    )
    units = 2 * gate_weight.shape[1]
    layer_out = mlp(copies, attended, norm_gain, weights, units)
    return attended.reshape(queries.shape), layer_out.reshape(queries.shape)


def solution(mesh):
    fine = Mesh(mesh.devices.reshape(SIZES), AXES)
    placed = (
        P(ROWS, None, BLK),
        P(ROWS, None, None, BLK),
        P(ROWS, None, None, BLK),
        P(ROWS, None, None, BLK),
        P(ROWS),
        P(ROWS, None),
        P(ROWS),
        P(BLK),
        P(BLK, ROWS),
        P(BLK, ROWS),
        P(ROWS, BLK),
    )
    return jax.shard_map(
        on_device,
        mesh=fine,
        in_specs=placed,
        out_specs=(P(ROWS, None, BLK), P(ROWS, None, BLK)),
        check_vma=False,
    )
```

```python
import math

import jax
import jax.numpy as jnp
from jax import lax
from jax.experimental import pallas as pl
from jax.experimental.pallas import tpu as pltpu
from jax.sharding import Mesh
from jax.sharding import PartitionSpec as P

GQ = 8
HD = 128
PAGE = 16
CAP = 2

AXES = ("ylo", "x", "zhi", "zlo", "yhi", "core")
SIZES = (2, 4, 4, 4, 2, 2)
BLK = ("ylo", "x")
ROWS = ("zhi", "zlo", "yhi", "core")
NEAR = ("zlo", "yhi", "core")
MID = ("zlo", "yhi")
SWAP = [(0, 1), (1, 0)]

epsilon = 1e-05


def spread(part, axes):
    count = lax.axis_size(axes)
    copies = jnp.broadcast_to(part[None], (count,) + part.shape)
    arrived = lax.all_to_all(copies, axes, split_axis=0, concat_axis=0, tiled=True)
    return arrived.reshape((count * part.shape[0],) + part.shape[1:])


def collect(parts, axes):
    arrived = lax.all_to_all(parts, axes, split_axis=0, concat_axis=0, tiled=True)
    return jnp.sum(arrived.astype(jnp.float32), axis=0)


def stack_heads(wide):
    count = wide.shape[1] // HD
    return jnp.concatenate([wide[:, g * HD : (g + 1) * HD] for g in range(count)], axis=0)


def head_rows(wide):
    return stack_heads(wide.astype(jnp.float32)).astype(jnp.bfloat16)


def scores(asked, keys):
    return (1.0 / math.sqrt(HD)) * lax.dot_general(
        asked, keys, (((1,), (1,)), ((), ())), preferred_element_type=jnp.float32
    )


def mix(weight, values):
    high = weight.astype(jnp.bfloat16)
    low = (weight - high.astype(jnp.float32)).astype(jnp.bfloat16)
    return jnp.dot(high, values, preferred_element_type=jnp.float32) + jnp.dot(
        low, values, preferred_element_type=jnp.float32
    )


def page_mask(token, step_count, seen):
    sign = jnp.where(token < step_count, 1.0, -1.0)
    offset = lax.broadcasted_iota(jnp.int32, seen.shape, 1) & (PAGE - 1)
    return sign * seen > offset.astype(jnp.float32)


def resident_kernel(asked_ref, resident_ref, new_ref, seen_ref, mixed_ref, peak_ref, total_ref):
    tokens, columns = asked_ref.shape
    width = columns - HD
    step_count = tokens // 2
    queries = width // HD * tokens
    token = lax.broadcasted_iota(jnp.int32, (queries, 1), 0) & (tokens - 1)
    asked = head_rows(asked_ref[:, :width])
    pages = resident_ref.shape[0]
    keys = resident_ref[:, 0].reshape(pages * PAGE, HD)
    values = resident_ref[:, 1].reshape(pages * PAGE, HD)
    mask = page_mask(token, step_count, seen_ref[...])
    score = jnp.where(mask, scores(asked, keys), -1e30)
    fresh = scores(asked, new_ref[0])
    other = lax.broadcasted_iota(jnp.int32, (1, fresh.shape[1]), 1)
    start = jnp.where(token < step_count, 0, step_count)
    fresh = jnp.where((other >= start) & (other <= token), fresh, -1e30)
    peak = jnp.maximum(
        jnp.max(score, axis=1, keepdims=True), jnp.max(fresh, axis=1, keepdims=True)
    )
    weight = jnp.exp(score - peak)
    fresh_weight = jnp.exp(fresh - peak)
    total = jnp.sum(weight, axis=1, keepdims=True) + jnp.sum(fresh_weight, axis=1, keepdims=True)
    mixed_ref[...] = mix(weight, values) + mix(fresh_weight, new_ref[1])
    peak_ref[...] = jnp.broadcast_to(peak, peak_ref.shape)
    total_ref[...] = jnp.broadcast_to(total, total_ref.shape)


def attend_kernel(far_ref, *refs):
    far = far_ref[0]
    pages_ref, mixed_ref, peak_ref, total_ref, out_ref = refs[-5:]
    asked_of = [ref[...] for ref in refs[:-5]]
    owners = len(asked_of)
    tokens, columns = asked_of[0].shape
    width = columns - HD
    heads = width // HD
    queries = heads * tokens
    token = lax.broadcasted_iota(jnp.int32, (queries, 1), 0) & (tokens - 1)
    senders, landed = pages_ref.shape[0], pages_ref.shape[1]
    slots = landed // owners
    key_count = senders * slots * PAGE
    place = lax.broadcasted_iota(jnp.int32, (HD, key_count), 1) // PAGE + far * (senders * slots)
    expand = (lax.broadcasted_iota(jnp.int32, (HD, key_count), 0) == place).astype(jnp.float32)
    expand = expand.astype(jnp.bfloat16)
    lane = lax.broadcasted_iota(jnp.int32, (tokens, HD), 1)
    for flip in range(owners):
        owner = far ^ flip
        table = asked_of[flip][:, width:]
        seen = jnp.dot(table, expand, preferred_element_type=jnp.float32)[0:1]
        asked = head_rows(asked_of[flip][:, :width])
        mine = pages_ref[:, pl.ds(owner * slots, slots)]
        keys = mine[:, :, 0].reshape(key_count, HD)
        values = mine[:, :, 1].reshape(key_count, HD)
        mask = page_mask(token, tokens // 2, seen)
        score = jnp.where(mask, scores(asked, keys), -1e30)
        peak = jnp.max(score, axis=1, keepdims=True)
        weight = jnp.where(mask, jnp.exp(score - peak), 0.0)
        total = jnp.sum(weight, axis=1, keepdims=True)
        mixed = mix(weight, values)
        own_peak = peak_ref[:, :1]
        top = jnp.maximum(peak, own_peak) if flip == 0 else peak
        top = top.astype(jnp.bfloat16).astype(jnp.float32)
        here = jnp.where(total > 0.0, jnp.exp(jnp.minimum(peak - top, 80.0)), 0.0)
        total = here * total
        mixed = here * mixed
        if flip == 0:
            own = jnp.exp(jnp.minimum(own_peak - top, 80.0))
            total = total + own * total_ref[:, :1]
            mixed = mixed + own * mixed_ref[...]
        mixed = mixed / jnp.where(total > 0.0, total, 1.0)
        total_high = total.astype(jnp.bfloat16).astype(jnp.float32)
        total_low = total - total_high
        stats = jnp.zeros((tokens, HD), jnp.float32)
        for g in range(heads):
            rows = slice(g * tokens, (g + 1) * tokens)
            stats = jnp.where(lane == g, top[rows], stats)
            stats = jnp.where(lane == heads + g, total_high[rows], stats)
            stats = jnp.where(lane == 2 * heads + g, total_low[rows], stats)
        line = jnp.concatenate(
            [mixed[g * tokens : (g + 1) * tokens] for g in range(heads)] + [stats], axis=1
        ).astype(jnp.bfloat16)
        for copy in range(out_ref.shape[0]):
            out_ref[copy, owner] = line


def merge_kernel(far_ref, parts_ref, copies_ref, attended_ref):
    sources, owners, tokens, columns = parts_ref.shape
    width = columns - HD
    heads = width // HD
    count = owners * tokens
    parts = [parts_ref[i].reshape(count, columns) for i in range(sources)]
    stats = [part[:, width:].astype(jnp.float32) for part in parts]
    peaks = [stat[:, :heads] for stat in stats]
    totals = [stat[:, heads : 2 * heads] + stat[:, 2 * heads : 3 * heads] for stat in stats]
    top = peaks[0]
    for peak in peaks[1:]:
        top = jnp.maximum(top, peak)
    shares = [total * jnp.exp(peak - top) for peak, total in zip(peaks, totals)]
    whole = shares[0]
    for share in shares[1:]:
        whole = whole + share
    shares = [share / whole for share in shares]
    blocks = []
    for g in range(heads):
        block = jnp.zeros((count, HD), jnp.float32)
        for part, share in zip(parts, shares):
            block = block + share[:, g : g + 1] * part[:, g * HD : (g + 1) * HD].astype(jnp.float32)
        blocks.append(block)
    merged = jnp.concatenate(blocks, axis=1)
    line = merged.astype(jnp.bfloat16)
    for copy in range(copies_ref.shape[0]):
        copies_ref[copy] = line
    own = merged[:tokens]
    for owner in range(1, owners):
        own = jnp.where(far_ref[0] == owner, merged[owner * tokens : (owner + 1) * tokens], own)
    attended_ref[...] = own.astype(jnp.bfloat16)


def attention(
    queries, new_entries, resident, swap_area, swap_dest, page_table, lengths, weights
):
    owners = lax.axis_size(ROWS)
    far_count = lax.axis_size("zhi")
    near_count = lax.axis_size(NEAR)
    mid_count = lax.axis_size(MID)
    far = lax.axis_index("zhi").astype(jnp.int32).reshape(1)
    rows_here, step_count, width = queries.shape
    tokens = rows_here * step_count
    pages_row = page_table.shape[1]
    pages_here = resident.shape[0]

    first = jnp.arange(pages_row, dtype=jnp.int32)[None, :] * PAGE
    seen = jnp.clip(lengths[:, None] - first, 0, PAGE) * jnp.array([[1], [-1]], jnp.int32)
    entries = jnp.arange(pages_here + owners * CAP, dtype=jnp.int32)
    named = page_table[:, :, None] == entries[None, None, :]
    seen = jnp.sum(jnp.where(named, seen[:, :, None], 0), axis=(0, 1)).astype(jnp.float32)
    table = jnp.pad(seen[None, pages_here:].astype(jnp.bfloat16), ((0, tokens - 1), (0, 0)))
    asked = jnp.concatenate([queries.reshape(tokens, width), table], axis=1)
    asked = [asked] + [
        lax.ppermute(asked, "zhi", [(i, i ^ flip) for i in range(far_count)])
        for flip in range(1, far_count)
    ]
    seen_here = jnp.repeat(seen[:pages_here], PAGE)[None, :]

    swap_count = swap_area.shape[0]
    page_width = swap_area.shape[1] * swap_area.shape[2] * swap_area.shape[3]
    same = swap_dest[:, None] == swap_dest[None, :]
    earlier = jnp.arange(swap_count)[None, :] < jnp.arange(swap_count)[:, None]
    page_rank = jnp.sum((same & earlier).astype(jnp.int32), axis=1)
    send_slot = (swap_dest % near_count) * (far_count * CAP) + (
        swap_dest // near_count
    ) * CAP + page_rank
    placement = (jnp.arange(owners * CAP, dtype=jnp.int32)[:, None] == send_slot[None, :]).astype(
        jnp.bfloat16
    )
    outgoing = jnp.dot(
        placement, swap_area.reshape(swap_count, page_width), preferred_element_type=jnp.float32
    ).astype(jnp.bfloat16)
    outgoing = outgoing.reshape((near_count, far_count * CAP) + swap_area.shape[1:])
    landed = lax.all_to_all(outgoing, NEAR, split_axis=0, concat_axis=0, tiled=True)

    fresh = new_entries.reshape(tokens, 2, HD).transpose(1, 0, 2)
    fresh = jnp.pad(fresh, ((0, 0), (0, HD - tokens), (0, 0)))
    whole = pl.BlockSpec(memory_space=pltpu.VMEM)
    scalar = pl.BlockSpec(memory_space=pltpu.SMEM)
    queries_here = width // HD * tokens
    square = jax.ShapeDtypeStruct((queries_here, HD), jnp.float32)
    found = pl.pallas_call(
        resident_kernel,
        out_shape=(square, square, square),
        in_specs=[whole] * 4,
        out_specs=(whole, whole, whole),
        compiler_params=pltpu.CompilerParams(vmem_limit_bytes=8 << 20),
        cost_estimate=pl.CostEstimate(
            flops=6 * queries_here * HD * pages_here * PAGE,
            bytes_accessed=2 * resident.size,
            transcendentals=queries_here * pages_here * PAGE,
        ),
    )(asked[0], resident, fresh, seen_here)
    found, weights = lax.optimization_barrier((found, weights))
    weights = join_weights(*weights)
    parts = pl.pallas_call(
        attend_kernel,
        out_shape=jax.ShapeDtypeStruct((far_count, far_count, tokens, width + HD), jnp.bfloat16),
        in_specs=[scalar] + [whole] * (far_count + 4),
        out_specs=whole,
        compiler_params=pltpu.CompilerParams(vmem_limit_bytes=12 << 20),
    )(far, *asked, landed, *found)
    parts = lax.all_to_all(parts, "zhi", split_axis=0, concat_axis=0, tiled=True)
    parts, weights = lax.optimization_barrier((parts, weights))
    copies, attended = pl.pallas_call(
        merge_kernel,
        out_shape=(
            jax.ShapeDtypeStruct((mid_count, far_count * tokens, width), jnp.bfloat16),
            jax.ShapeDtypeStruct((tokens, width), jnp.bfloat16),
        ),
        in_specs=[scalar, whole],
        out_specs=(whole, whole),
        compiler_params=pltpu.CompilerParams(vmem_limit_bytes=6 << 20),
    )(far, parts)
    return copies, attended, weights


def join_weights(gate_weight, up_weight, down_weight):
    units, width = down_weight.shape
    gate, up = gate_weight.T, up_weight.T
    there = lax.ppermute(jnp.concatenate([gate, up, down_weight], axis=0), "core", SWAP)
    gap = jnp.zeros((128, width), gate_weight.dtype)
    wide = jnp.concatenate([gate, there[:units], up, there[units : 2 * units], gap], axis=0)
    return wide, jnp.concatenate([down_weight, there[2 * units :]], axis=0)


def gated_parts(tokens, norm_gain, weights, units):
    wide = tokens.astype(jnp.float32)
    squares = jnp.sum(wide * wide, axis=1, keepdims=True)
    squares_high = squares.astype(jnp.bfloat16).astype(jnp.float32)
    normed = (wide * norm_gain.astype(jnp.float32)[None, :]).astype(jnp.bfloat16)
    both = lax.dot_general(
        normed, weights, (((1,), (1,)), ((), ())), preferred_element_type=jnp.float32
    )
    column = jnp.arange(both.shape[1], dtype=jnp.int32)[None, :]
    both = jnp.where(column == 2 * units, squares_high, both)
    both = jnp.where(column == 2 * units + 1, squares - squares_high, both)
    return both.astype(jnp.bfloat16)


def mlp(copies, attended, norm_gain, weights, units):
    wide_weight, down_weight = weights
    tokens_here, width = attended.shape
    far = lax.axis_size("zhi")
    mid = lax.axis_size(MID)
    blk = lax.axis_size(BLK)
    own = lax.all_to_all(copies, MID, split_axis=0, concat_axis=0, tiled=True).reshape(-1, width)
    parts = gated_parts(own, norm_gain, wide_weight, units)
    summed = collect(parts.reshape(blk, own.shape[0] // blk, parts.shape[1]), BLK)
    square_sum = summed[:, 2 * units : 2 * units + 1] + summed[:, 2 * units + 1 : 2 * units + 2]
    factor = lax.rsqrt(square_sum / (width * blk) + epsilon)
    gate_sum = summed[:, :units]
    up_sum = summed[:, units : 2 * units]
    hidden = (jax.nn.silu(factor * gate_sum) * (factor * up_sum)).astype(jnp.bfloat16)
    hidden = spread(hidden, BLK)
    kept = jnp.dot(hidden, down_weight, preferred_element_type=jnp.float32).astype(jnp.bfloat16)
    kept = collect(kept.reshape(mid, far * tokens_here, width), MID).astype(jnp.bfloat16)
    down_sum = collect(kept.reshape(far, tokens_here, width), "zhi")
    return (attended.astype(jnp.float32) + down_sum).astype(jnp.bfloat16)


def on_device(
    queries,
    new_entries,
    resident,
    swap_area,
    swap_dest,
    page_table,
    lengths,
    norm_gain,
    gate_weight,
    up_weight,
    down_weight,
):
    weights = (gate_weight, up_weight, down_weight)
    copies, attended, weights = attention(
        queries, new_entries, resident, swap_area, swap_dest, page_table, lengths, weights
    )
    units = 2 * gate_weight.shape[1]
    layer_out = mlp(copies, attended, norm_gain, weights, units)
    return attended.reshape(queries.shape), layer_out.reshape(queries.shape)


def solution(mesh):
    fine = Mesh(mesh.devices.reshape(SIZES), AXES)
    placed = (
        P(ROWS, None, BLK),
        P(ROWS, None, None, BLK),
        P(ROWS, None, None, BLK),
        P(ROWS, None, None, BLK),
        P(ROWS),
        P(ROWS, None),
        P(ROWS),
        P(BLK),
        P(BLK, ROWS),
        P(BLK, ROWS),
        P(ROWS, BLK),
    )
    return jax.shard_map(
        on_device,
        mesh=fine,
        in_specs=placed,
        out_specs=(P(ROWS, None, BLK), P(ROWS, None, BLK)),
        check_vma=False,
    )
```

```python
import math

import jax
import jax.numpy as jnp
from jax import lax
from jax.experimental import pallas as pl
from jax.experimental.pallas import tpu as pltpu
from jax.sharding import Mesh
from jax.sharding import PartitionSpec as P

GQ = 8
HD = 128
PAGE = 16
CAP = 2

AXES = ("ylo", "x", "zhi", "zlo", "yhi", "core")
SIZES = (2, 4, 4, 4, 2, 2)
BLK = ("ylo", "x")
ROWS = ("zhi", "zlo", "yhi", "core")
NEAR = ("zlo", "yhi", "core")
MID = ("zlo", "yhi")
SWAP = [(0, 1), (1, 0)]

epsilon = 1e-05


def spread(part, axes):
    count = lax.axis_size(axes)
    copies = jnp.broadcast_to(part[None], (count,) + part.shape)
    arrived = lax.all_to_all(copies, axes, split_axis=0, concat_axis=0, tiled=True)
    return arrived.reshape((count * part.shape[0],) + part.shape[1:])


def collect(parts, axes):
    arrived = lax.all_to_all(parts, axes, split_axis=0, concat_axis=0, tiled=True)
    return jnp.sum(arrived.astype(jnp.float32), axis=0)


def stack_heads(wide):
    count = wide.shape[1] // HD
    return jnp.concatenate([wide[:, g * HD : (g + 1) * HD] for g in range(count)], axis=0)


def head_rows(wide):
    return stack_heads(wide.astype(jnp.float32)).astype(jnp.bfloat16)


def scores(asked, keys):
    return (1.0 / math.sqrt(HD)) * lax.dot_general(
        asked, keys, (((1,), (1,)), ((), ())), preferred_element_type=jnp.float32
    )


def mix(weight, values):
    high = weight.astype(jnp.bfloat16)
    low = (weight - high.astype(jnp.float32)).astype(jnp.bfloat16)
    return jnp.dot(high, values, preferred_element_type=jnp.float32) + jnp.dot(
        low, values, preferred_element_type=jnp.float32
    )


def page_mask(token, step_count, seen):
    sign = jnp.where(token < step_count, 1.0, -1.0)
    offset = lax.broadcasted_iota(jnp.int32, seen.shape, 1) & (PAGE - 1)
    return sign * seen > offset.astype(jnp.float32)


def resident_kernel(asked_ref, resident_ref, new_ref, seen_ref, mixed_ref, peak_ref, total_ref):
    tokens, columns = asked_ref.shape
    width = columns - HD
    step_count = tokens // 2
    queries = width // HD * tokens
    token = lax.broadcasted_iota(jnp.int32, (queries, 1), 0) & (tokens - 1)
    asked = head_rows(asked_ref[:, :width])
    pages = resident_ref.shape[0]
    keys = resident_ref[:, 0].reshape(pages * PAGE, HD)
    values = resident_ref[:, 1].reshape(pages * PAGE, HD)
    mask = page_mask(token, step_count, seen_ref[...])
    score = jnp.where(mask, scores(asked, keys), -1e30)
    fresh = scores(asked, new_ref[0])
    other = lax.broadcasted_iota(jnp.int32, (1, fresh.shape[1]), 1)
    start = jnp.where(token < step_count, 0, step_count)
    fresh = jnp.where((other >= start) & (other <= token), fresh, -1e30)
    peak = jnp.maximum(
        jnp.max(score, axis=1, keepdims=True), jnp.max(fresh, axis=1, keepdims=True)
    )
    weight = jnp.exp(score - peak)
    fresh_weight = jnp.exp(fresh - peak)
    total = jnp.sum(weight, axis=1, keepdims=True) + jnp.sum(fresh_weight, axis=1, keepdims=True)
    mixed_ref[...] = mix(weight, values) + mix(fresh_weight, new_ref[1])
    peak_ref[...] = jnp.broadcast_to(peak, peak_ref.shape)
    total_ref[...] = jnp.broadcast_to(total, total_ref.shape)


def attend_kernel(far_ref, *refs):
    far = far_ref[0]
    pages_ref, mixed_ref, peak_ref, total_ref, out_ref = refs[-5:]
    asked_of = [ref[...] for ref in refs[:-5]]
    owners = len(asked_of)
    tokens, columns = asked_of[0].shape
    width = columns - HD
    heads = width // HD
    queries = heads * tokens
    token = lax.broadcasted_iota(jnp.int32, (queries, 1), 0) & (tokens - 1)
    senders, landed = pages_ref.shape[0], pages_ref.shape[1]
    slots = landed // owners
    key_count = senders * slots * PAGE
    place = lax.broadcasted_iota(jnp.int32, (HD, key_count), 1) // PAGE + far * (senders * slots)
    expand = (lax.broadcasted_iota(jnp.int32, (HD, key_count), 0) == place).astype(jnp.float32)
    expand = expand.astype(jnp.bfloat16)
    lane = lax.broadcasted_iota(jnp.int32, (tokens, HD), 1)
    for flip in range(owners):
        owner = far ^ flip
        table = asked_of[flip][:, width:]
        seen = jnp.dot(table, expand, preferred_element_type=jnp.float32)[0:1]
        asked = head_rows(asked_of[flip][:, :width])
        mine = pages_ref[:, pl.ds(owner * slots, slots)]
        keys = mine[:, :, 0].reshape(key_count, HD)
        values = mine[:, :, 1].reshape(key_count, HD)
        mask = page_mask(token, tokens // 2, seen)
        score = jnp.where(mask, scores(asked, keys), -1e30)
        peak = jnp.max(score, axis=1, keepdims=True)
        weight = jnp.where(mask, jnp.exp(score - peak), 0.0)
        total = jnp.sum(weight, axis=1, keepdims=True)
        mixed = mix(weight, values)
        own_peak = peak_ref[:, :1]
        top = jnp.maximum(peak, own_peak) if flip == 0 else peak
        top = top.astype(jnp.bfloat16).astype(jnp.float32)
        here = jnp.where(total > 0.0, jnp.exp(jnp.minimum(peak - top, 80.0)), 0.0)
        total = here * total
        mixed = here * mixed
        if flip == 0:
            own = jnp.exp(jnp.minimum(own_peak - top, 80.0))
            total = total + own * total_ref[:, :1]
            mixed = mixed + own * mixed_ref[...]
        mixed = mixed / jnp.where(total > 0.0, total, 1.0)
        total_high = total.astype(jnp.bfloat16).astype(jnp.float32)
        total_low = total - total_high
        stats = jnp.zeros((tokens, HD), jnp.float32)
        for g in range(heads):
            rows = slice(g * tokens, (g + 1) * tokens)
            stats = jnp.where(lane == g, top[rows], stats)
            stats = jnp.where(lane == heads + g, total_high[rows], stats)
            stats = jnp.where(lane == 2 * heads + g, total_low[rows], stats)
        line = jnp.concatenate(
            [mixed[g * tokens : (g + 1) * tokens] for g in range(heads)] + [stats], axis=1
        ).astype(jnp.bfloat16)
        for copy in range(out_ref.shape[0]):
            out_ref[copy, owner] = line


def merge_kernel(far_ref, parts_ref, copies_ref, attended_ref):
    sources, owners, tokens, columns = parts_ref.shape
    width = columns - HD
    heads = width // HD
    count = owners * tokens
    parts = [parts_ref[i].reshape(count, columns) for i in range(sources)]
    stats = [part[:, width:].astype(jnp.float32) for part in parts]
    peaks = [stat[:, :heads] for stat in stats]
    totals = [stat[:, heads : 2 * heads] + stat[:, 2 * heads : 3 * heads] for stat in stats]
    top = peaks[0]
    for peak in peaks[1:]:
        top = jnp.maximum(top, peak)
    shares = [total * jnp.exp(peak - top) for peak, total in zip(peaks, totals)]
    whole = shares[0]
    for share in shares[1:]:
        whole = whole + share
    shares = [share / whole for share in shares]
    blocks = []
    for g in range(heads):
        block = jnp.zeros((count, HD), jnp.float32)
        for part, share in zip(parts, shares):
            block = block + share[:, g : g + 1] * part[:, g * HD : (g + 1) * HD].astype(jnp.float32)
        blocks.append(block)
    merged = jnp.concatenate(blocks, axis=1)
    line = merged.astype(jnp.bfloat16)
    for copy in range(copies_ref.shape[0]):
        copies_ref[copy] = line
    own = merged[:tokens]
    for owner in range(1, owners):
        own = jnp.where(far_ref[0] == owner, merged[owner * tokens : (owner + 1) * tokens], own)
    attended_ref[...] = own.astype(jnp.bfloat16)


def attention(
    queries, new_entries, resident, swap_area, swap_dest, page_table, lengths, weights
):
    owners = lax.axis_size(ROWS)
    far_count = lax.axis_size("zhi")
    near_count = lax.axis_size(NEAR)
    mid_count = lax.axis_size(MID)
    far = lax.axis_index("zhi").astype(jnp.int32).reshape(1)
    rows_here, step_count, width = queries.shape
    tokens = rows_here * step_count
    pages_row = page_table.shape[1]
    pages_here = resident.shape[0]

    first = jnp.arange(pages_row, dtype=jnp.int32)[None, :] * PAGE
    seen = jnp.clip(lengths[:, None] - first, 0, PAGE) * jnp.array([[1], [-1]], jnp.int32)
    entries = jnp.arange(pages_here + owners * CAP, dtype=jnp.int32)
    named = page_table[:, :, None] == entries[None, None, :]
    seen = jnp.sum(jnp.where(named, seen[:, :, None], 0), axis=(0, 1)).astype(jnp.float32)
    table = jnp.pad(seen[None, pages_here:].astype(jnp.bfloat16), ((0, tokens - 1), (0, 0)))
    asked = jnp.concatenate([queries.reshape(tokens, width), table], axis=1)
    asked = [asked] + [
        lax.ppermute(asked, "zhi", [(i, i ^ flip) for i in range(far_count)])
        for flip in range(1, far_count)
    ]
    seen_here = jnp.repeat(seen[:pages_here], PAGE)[None, :]

    swap_count = swap_area.shape[0]
    same = swap_dest[:, None] == swap_dest[None, :]
    earlier = jnp.arange(swap_count)[None, :] < jnp.arange(swap_count)[:, None]
    page_rank = jnp.sum((same & earlier).astype(jnp.int32), axis=1)
    send_slot = (swap_dest % near_count) * (far_count * CAP) + (
        swap_dest // near_count
    ) * CAP + page_rank
    slots = jnp.arange(owners * CAP, dtype=jnp.int32)[:, None]
    pages = jnp.arange(swap_count, dtype=jnp.int32)[None, :]
    source = jnp.sum(jnp.where(slots == send_slot[None, :], pages, 0), axis=1)
    outgoing = swap_area.at[source].get(mode="promise_in_bounds")
    outgoing = outgoing.reshape((near_count, far_count * CAP) + swap_area.shape[1:])
    landed = lax.all_to_all(outgoing, NEAR, split_axis=0, concat_axis=0, tiled=True)

    fresh = new_entries.reshape(tokens, 2, HD).transpose(1, 0, 2)
    fresh = jnp.pad(fresh, ((0, 0), (0, HD - tokens), (0, 0)))
    whole = pl.BlockSpec(memory_space=pltpu.VMEM)
    scalar = pl.BlockSpec(memory_space=pltpu.SMEM)
    queries_here = width // HD * tokens
    square = jax.ShapeDtypeStruct((queries_here, HD), jnp.float32)
    found = pl.pallas_call(
        resident_kernel,
        out_shape=(square, square, square),
        in_specs=[whole] * 4,
        out_specs=(whole, whole, whole),
        compiler_params=pltpu.CompilerParams(vmem_limit_bytes=8 << 20),
        cost_estimate=pl.CostEstimate(
            flops=6 * queries_here * HD * pages_here * PAGE,
            bytes_accessed=2 * resident.size,
            transcendentals=queries_here * pages_here * PAGE,
        ),
    )(asked[0], resident, fresh, seen_here)
    found, weights = lax.optimization_barrier((found, weights))
    weights = join_weights(*weights)
    parts = pl.pallas_call(
        attend_kernel,
        out_shape=jax.ShapeDtypeStruct((far_count, far_count, tokens, width + HD), jnp.bfloat16),
        in_specs=[scalar] + [whole] * (far_count + 4),
        out_specs=whole,
        compiler_params=pltpu.CompilerParams(vmem_limit_bytes=12 << 20),
    )(far, *asked, landed, *found)
    parts = lax.all_to_all(parts, "zhi", split_axis=0, concat_axis=0, tiled=True)
    parts, weights = lax.optimization_barrier((parts, weights))
    copies, attended = pl.pallas_call(
        merge_kernel,
        out_shape=(
            jax.ShapeDtypeStruct((mid_count, far_count * tokens, width), jnp.bfloat16),
            jax.ShapeDtypeStruct((tokens, width), jnp.bfloat16),
        ),
        in_specs=[scalar, whole],
        out_specs=(whole, whole),
        compiler_params=pltpu.CompilerParams(vmem_limit_bytes=6 << 20),
    )(far, parts)
    return copies, attended, weights


def join_weights(gate_weight, up_weight, down_weight):
    units, width = down_weight.shape
    gate, up = gate_weight.T, up_weight.T
    there = lax.ppermute(jnp.concatenate([gate, up, down_weight], axis=0), "core", SWAP)
    own = jnp.concatenate([gate, up], axis=0)
    down = jnp.concatenate([down_weight, there[2 * units :]], axis=0)
    return own, there[: 2 * units], down


def gated_parts(tokens, norm_gain, weights):
    wide = tokens.astype(jnp.float32)
    squares = jnp.sum(wide * wide, axis=1, keepdims=True)
    squares_high = squares.astype(jnp.bfloat16).astype(jnp.float32)
    normed = (wide * norm_gain.astype(jnp.float32)[None, :]).astype(jnp.bfloat16)
    blocks = [
        lax.dot_general(
            normed, weight, (((1,), (1,)), ((), ())), preferred_element_type=jnp.float32
        ).astype(jnp.bfloat16)
        for weight in weights
    ]
    column = jnp.arange(128, dtype=jnp.int32)[None, :]
    last = jnp.where(column == 0, squares_high, squares - squares_high).astype(jnp.bfloat16)
    return jnp.concatenate(blocks + [last], axis=1)


def mlp(copies, attended, norm_gain, weights, units):
    *wide_weights, down_weight = weights
    tokens_here, width = attended.shape
    far = lax.axis_size("zhi")
    mid = lax.axis_size(MID)
    blk = lax.axis_size(BLK)
    own = lax.all_to_all(copies, MID, split_axis=0, concat_axis=0, tiled=True).reshape(-1, width)
    parts = gated_parts(own, norm_gain, wide_weights)
    summed = collect(parts.reshape(blk, own.shape[0] // blk, parts.shape[1]), BLK)
    square_sum = summed[:, 4 * units : 4 * units + 1] + summed[:, 4 * units + 1 : 4 * units + 2]
    factor = lax.rsqrt(square_sum / (width * blk) + epsilon)
    hidden = []
    for first in (0, 2 * units):
        gate_sum = summed[:, first : first + units]
        up_sum = summed[:, first + units : first + 2 * units]
        hidden.append((jax.nn.silu(factor * gate_sum) * (factor * up_sum)).astype(jnp.bfloat16))
    hidden = jnp.concatenate(hidden, axis=1)
    hidden = spread(hidden, BLK)
    kept = jnp.dot(hidden, down_weight, preferred_element_type=jnp.float32).astype(jnp.bfloat16)
    kept = collect(kept.reshape(mid, far * tokens_here, width), MID).astype(jnp.bfloat16)
    down_sum = collect(kept.reshape(far, tokens_here, width), "zhi")
    return (attended.astype(jnp.float32) + down_sum).astype(jnp.bfloat16)


def on_device(
    queries,
    new_entries,
    resident,
    swap_area,
    swap_dest,
    page_table,
    lengths,
    norm_gain,
    gate_weight,
    up_weight,
    down_weight,
):
    weights = (gate_weight, up_weight, down_weight)
    copies, attended, weights = attention(
        queries, new_entries, resident, swap_area, swap_dest, page_table, lengths, weights
    )
    units = gate_weight.shape[1]
    layer_out = mlp(copies, attended, norm_gain, weights, units)
    return attended.reshape(queries.shape), layer_out.reshape(queries.shape)


def solution(mesh):
    fine = Mesh(mesh.devices.reshape(SIZES), AXES)
    placed = (
        P(ROWS, None, BLK),
        P(ROWS, None, None, BLK),
        P(ROWS, None, None, BLK),
        P(ROWS, None, None, BLK),
        P(ROWS),
        P(ROWS, None),
        P(ROWS),
        P(BLK),
        P(BLK, ROWS),
        P(BLK, ROWS),
        P(ROWS, BLK),
    )
    return jax.shard_map(
        on_device,
        mesh=fine,
        in_specs=placed,
        out_specs=(P(ROWS, None, BLK), P(ROWS, None, BLK)),
        check_vma=False,
    )
```

```python
import math

import jax
import jax.numpy as jnp
from jax import lax
from jax.experimental import pallas as pl
from jax.experimental.pallas import tpu as pltpu
from jax.sharding import Mesh
from jax.sharding import PartitionSpec as P

GQ = 8
HD = 128
PAGE = 16
CAP = 2

AXES = ("ylo", "x", "zhi", "zlo", "yhi", "core")
SIZES = (2, 4, 4, 4, 2, 2)
BLK = ("ylo", "x")
ROWS = ("zhi", "zlo", "yhi", "core")
NEAR = ("zlo", "yhi", "core")
MID = ("zlo", "yhi")
SWAP = [(0, 1), (1, 0)]

epsilon = 1e-05


def spread(part, axes):
    count = lax.axis_size(axes)
    copies = jnp.broadcast_to(part[None], (count,) + part.shape)
    arrived = lax.all_to_all(copies, axes, split_axis=0, concat_axis=0, tiled=True)
    return arrived.reshape((count * part.shape[0],) + part.shape[1:])


def collect(parts, axes):
    arrived = lax.all_to_all(parts, axes, split_axis=0, concat_axis=0, tiled=True)
    return jnp.sum(arrived.astype(jnp.float32), axis=0)


def stack_heads(wide):
    count = wide.shape[1] // HD
    return jnp.concatenate([wide[:, g * HD : (g + 1) * HD] for g in range(count)], axis=0)


def head_rows(wide):
    return stack_heads(wide.astype(jnp.float32)).astype(jnp.bfloat16)


def scores(asked, keys):
    return (1.0 / math.sqrt(HD)) * lax.dot_general(
        asked, keys, (((1,), (1,)), ((), ())), preferred_element_type=jnp.float32
    )


def mix(weight, values):
    high = weight.astype(jnp.bfloat16)
    low = (weight - high.astype(jnp.float32)).astype(jnp.bfloat16)
    return jnp.dot(high, values, preferred_element_type=jnp.float32) + jnp.dot(
        low, values, preferred_element_type=jnp.float32
    )


def page_mask(token, step_count, seen):
    sign = jnp.where(token < step_count, 1.0, -1.0)
    offset = lax.broadcasted_iota(jnp.int32, seen.shape, 1) & (PAGE - 1)
    return sign * seen > offset.astype(jnp.float32)


def resident_kernel(asked_ref, resident_ref, new_ref, seen_ref, mixed_ref, peak_ref, total_ref):
    tokens, columns = asked_ref.shape
    width = columns - HD
    step_count = tokens // 2
    queries = width // HD * tokens
    token = lax.broadcasted_iota(jnp.int32, (queries, 1), 0) & (tokens - 1)
    asked = head_rows(asked_ref[:, :width])
    pages = resident_ref.shape[0]
    keys = resident_ref[:, 0].reshape(pages * PAGE, HD)
    values = resident_ref[:, 1].reshape(pages * PAGE, HD)
    mask = page_mask(token, step_count, seen_ref[...])
    score = jnp.where(mask, scores(asked, keys), -1e30)
    fresh = scores(asked, new_ref[0])
    other = lax.broadcasted_iota(jnp.int32, (1, fresh.shape[1]), 1)
    start = jnp.where(token < step_count, 0, step_count)
    fresh = jnp.where((other >= start) & (other <= token), fresh, -1e30)
    peak = jnp.maximum(
        jnp.max(score, axis=1, keepdims=True), jnp.max(fresh, axis=1, keepdims=True)
    )
    weight = jnp.exp(score - peak)
    fresh_weight = jnp.exp(fresh - peak)
    total = jnp.sum(weight, axis=1, keepdims=True) + jnp.sum(fresh_weight, axis=1, keepdims=True)
    mixed_ref[...] = mix(weight, values) + mix(fresh_weight, new_ref[1])
    peak_ref[...] = jnp.broadcast_to(peak, peak_ref.shape)
    total_ref[...] = jnp.broadcast_to(total, total_ref.shape)


def attend_kernel(far_ref, *refs):
    far = far_ref[0]
    pages_ref, mixed_ref, peak_ref, total_ref, out_ref = refs[-5:]
    asked_of = [ref[...] for ref in refs[:-5]]
    owners = len(asked_of)
    tokens, columns = asked_of[0].shape
    width = columns - HD
    heads = width // HD
    queries = heads * tokens
    token = lax.broadcasted_iota(jnp.int32, (queries, 1), 0) & (tokens - 1)
    senders, landed = pages_ref.shape[0], pages_ref.shape[1]
    slots = landed // owners
    key_count = senders * slots * PAGE
    place = lax.broadcasted_iota(jnp.int32, (HD, key_count), 1) // PAGE + far * (senders * slots)
    expand = (lax.broadcasted_iota(jnp.int32, (HD, key_count), 0) == place).astype(jnp.float32)
    expand = expand.astype(jnp.bfloat16)
    lane = lax.broadcasted_iota(jnp.int32, (tokens, HD), 1)
    for flip in range(owners):
        owner = far ^ flip
        table = asked_of[flip][:, width:]
        seen = jnp.dot(table, expand, preferred_element_type=jnp.float32)[0:1]
        asked = head_rows(asked_of[flip][:, :width])
        mine = pages_ref[:, pl.ds(owner * slots, slots)]
        keys = mine[:, :, 0].reshape(key_count, HD)
        values = mine[:, :, 1].reshape(key_count, HD)
        mask = page_mask(token, tokens // 2, seen)
        score = jnp.where(mask, scores(asked, keys), -1e30)
        peak = jnp.max(score, axis=1, keepdims=True)
        weight = jnp.where(mask, jnp.exp(score - peak), 0.0)
        total = jnp.sum(weight, axis=1, keepdims=True)
        mixed = mix(weight, values)
        own_peak = peak_ref[:, :1]
        top = jnp.maximum(peak, own_peak) if flip == 0 else peak
        top = top.astype(jnp.bfloat16).astype(jnp.float32)
        here = jnp.where(total > 0.0, jnp.exp(jnp.minimum(peak - top, 80.0)), 0.0)
        total = here * total
        mixed = here * mixed
        if flip == 0:
            own = jnp.exp(jnp.minimum(own_peak - top, 80.0))
            total = total + own * total_ref[:, :1]
            mixed = mixed + own * mixed_ref[...]
        mixed = mixed / jnp.where(total > 0.0, total, 1.0)
        total_high = total.astype(jnp.bfloat16).astype(jnp.float32)
        total_low = total - total_high
        stats = jnp.zeros((tokens, HD), jnp.float32)
        for g in range(heads):
            rows = slice(g * tokens, (g + 1) * tokens)
            stats = jnp.where(lane == g, top[rows], stats)
            stats = jnp.where(lane == heads + g, total_high[rows], stats)
            stats = jnp.where(lane == 2 * heads + g, total_low[rows], stats)
        line = jnp.concatenate(
            [mixed[g * tokens : (g + 1) * tokens] for g in range(heads)] + [stats], axis=1
        ).astype(jnp.bfloat16)
        for copy in range(out_ref.shape[0]):
            out_ref[copy, owner] = line


def merge_kernel(far_ref, parts_ref, copies_ref, attended_ref):
    sources, owners, tokens, columns = parts_ref.shape
    width = columns - HD
    heads = width // HD
    count = owners * tokens
    parts = [parts_ref[i].reshape(count, columns) for i in range(sources)]
    stats = [part[:, width:].astype(jnp.float32) for part in parts]
    peaks = [stat[:, :heads] for stat in stats]
    totals = [stat[:, heads : 2 * heads] + stat[:, 2 * heads : 3 * heads] for stat in stats]
    top = peaks[0]
    for peak in peaks[1:]:
        top = jnp.maximum(top, peak)
    shares = [total * jnp.exp(peak - top) for peak, total in zip(peaks, totals)]
    whole = shares[0]
    for share in shares[1:]:
        whole = whole + share
    shares = [share / whole for share in shares]
    blocks = []
    for g in range(heads):
        block = jnp.zeros((count, HD), jnp.float32)
        for part, share in zip(parts, shares):
            block = block + share[:, g : g + 1] * part[:, g * HD : (g + 1) * HD].astype(jnp.float32)
        blocks.append(block)
    merged = jnp.concatenate(blocks, axis=1)
    line = merged.astype(jnp.bfloat16)
    for copy in range(copies_ref.shape[0]):
        copies_ref[copy] = line
    own = merged[:tokens]
    for owner in range(1, owners):
        own = jnp.where(far_ref[0] == owner, merged[owner * tokens : (owner + 1) * tokens], own)
    attended_ref[...] = own.astype(jnp.bfloat16)


def attention(
    queries, new_entries, resident, swap_area, swap_dest, page_table, lengths, weights
):
    owners = lax.axis_size(ROWS)
    far_count = lax.axis_size("zhi")
    near_count = lax.axis_size(NEAR)
    mid_count = lax.axis_size(MID)
    far = lax.axis_index("zhi").astype(jnp.int32).reshape(1)
    rows_here, step_count, width = queries.shape
    tokens = rows_here * step_count
    pages_row = page_table.shape[1]
    pages_here = resident.shape[0]

    first = jnp.arange(pages_row, dtype=jnp.int32)[None, :] * PAGE
    seen = jnp.clip(lengths[:, None] - first, 0, PAGE) * jnp.array([[1], [-1]], jnp.int32)
    entries = jnp.arange(pages_here + owners * CAP, dtype=jnp.int32)
    named = page_table[:, :, None] == entries[None, None, :]
    seen = jnp.sum(jnp.where(named, seen[:, :, None], 0), axis=(0, 1)).astype(jnp.float32)
    table = jnp.pad(seen[None, pages_here:].astype(jnp.bfloat16), ((0, tokens - 1), (0, 0)))
    asked = jnp.concatenate([queries.reshape(tokens, width), table], axis=1)
    asked = [asked] + [
        lax.ppermute(asked, "zhi", [(i, i ^ flip) for i in range(far_count)])
        for flip in range(1, far_count)
    ]
    seen_here = jnp.repeat(seen[:pages_here], PAGE)[None, :]

    swap_count = swap_area.shape[0]
    same = swap_dest[:, None] == swap_dest[None, :]
    earlier = jnp.arange(swap_count)[None, :] < jnp.arange(swap_count)[:, None]
    page_rank = jnp.sum((same & earlier).astype(jnp.int32), axis=1)
    send_slot = (swap_dest % near_count) * (far_count * CAP) + (
        swap_dest // near_count
    ) * CAP + page_rank
    slots = jnp.arange(owners * CAP, dtype=jnp.int32)[:, None]
    pages = jnp.arange(swap_count, dtype=jnp.int32)[None, :]
    source = jnp.sum(jnp.where(slots == send_slot[None, :], pages, 0), axis=1)
    outgoing = swap_area.at[source].get(mode="promise_in_bounds")
    outgoing = outgoing.reshape((near_count, far_count * CAP) + swap_area.shape[1:])
    landed = lax.all_to_all(outgoing, NEAR, split_axis=0, concat_axis=0, tiled=True)

    fresh = new_entries.reshape(tokens, 2, HD).transpose(1, 0, 2)
    fresh = jnp.pad(fresh, ((0, 0), (0, HD - tokens), (0, 0)))
    whole = pl.BlockSpec(memory_space=pltpu.VMEM)
    scalar = pl.BlockSpec(memory_space=pltpu.SMEM)
    queries_here = width // HD * tokens
    square = jax.ShapeDtypeStruct((queries_here, HD), jnp.float32)
    found = pl.pallas_call(
        resident_kernel,
        out_shape=(square, square, square),
        in_specs=[whole] * 4,
        out_specs=(whole, whole, whole),
        compiler_params=pltpu.CompilerParams(vmem_limit_bytes=4 << 20),
        cost_estimate=pl.CostEstimate(
            flops=6 * queries_here * HD * pages_here * PAGE,
            bytes_accessed=2 * resident.size,
            transcendentals=queries_here * pages_here * PAGE,
        ),
    )(asked[0], resident, fresh, seen_here)
    found, weights = lax.optimization_barrier((found, weights))
    weights = join_weights(*weights)
    parts = pl.pallas_call(
        attend_kernel,
        out_shape=jax.ShapeDtypeStruct((far_count, far_count, tokens, width + HD), jnp.bfloat16),
        in_specs=[scalar] + [whole] * (far_count + 4),
        out_specs=whole,
        compiler_params=pltpu.CompilerParams(vmem_limit_bytes=6 << 20),
    )(far, *asked, landed, *found)
    parts = lax.all_to_all(parts, "zhi", split_axis=0, concat_axis=0, tiled=True)
    parts, weights = lax.optimization_barrier((parts, weights))
    copies, attended = pl.pallas_call(
        merge_kernel,
        out_shape=(
            jax.ShapeDtypeStruct((mid_count, far_count * tokens, width), jnp.bfloat16),
            jax.ShapeDtypeStruct((tokens, width), jnp.bfloat16),
        ),
        in_specs=[scalar, whole],
        out_specs=(whole, whole),
        compiler_params=pltpu.CompilerParams(vmem_limit_bytes=6 << 20),
    )(far, parts)
    return copies, attended, weights


def join_weights(gate_weight, up_weight, down_weight):
    units, width = down_weight.shape
    gate, up = gate_weight.T, up_weight.T
    there = lax.ppermute(jnp.concatenate([gate, up, down_weight], axis=0), "core", SWAP)
    own = jnp.concatenate([gate, up], axis=0)
    down = jnp.concatenate([down_weight, there[2 * units :]], axis=0)
    return own, there[: 2 * units], down


def gated_parts(tokens, norm_gain, weights):
    wide = tokens.astype(jnp.float32)
    squares = jnp.sum(wide * wide, axis=1, keepdims=True)
    squares_high = squares.astype(jnp.bfloat16).astype(jnp.float32)
    normed = (wide * norm_gain.astype(jnp.float32)[None, :]).astype(jnp.bfloat16)
    blocks = [
        lax.dot_general(
            normed, weight, (((1,), (1,)), ((), ())), preferred_element_type=jnp.float32
        ).astype(jnp.bfloat16)
        for weight in weights
    ]
    column = jnp.arange(128, dtype=jnp.int32)[None, :]
    last = jnp.where(column == 0, squares_high, squares - squares_high).astype(jnp.bfloat16)
    return jnp.concatenate(blocks + [last], axis=1)


def mlp(copies, attended, norm_gain, weights, units):
    *wide_weights, down_weight = weights
    tokens_here, width = attended.shape
    far = lax.axis_size("zhi")
    mid = lax.axis_size(MID)
    blk = lax.axis_size(BLK)
    own = lax.all_to_all(copies, MID, split_axis=0, concat_axis=0, tiled=True).reshape(-1, width)
    parts = gated_parts(own, norm_gain, wide_weights)
    summed = collect(parts.reshape(blk, own.shape[0] // blk, parts.shape[1]), BLK)
    square_sum = summed[:, 4 * units : 4 * units + 1] + summed[:, 4 * units + 1 : 4 * units + 2]
    factor = lax.rsqrt(square_sum / (width * blk) + epsilon)
    hidden = []
    for first in (0, 2 * units):
        gate_sum = summed[:, first : first + units]
        up_sum = summed[:, first + units : first + 2 * units]
        hidden.append((jax.nn.silu(factor * gate_sum) * (factor * up_sum)).astype(jnp.bfloat16))
    hidden = jnp.concatenate(hidden, axis=1)
    hidden = spread(hidden, BLK)
    kept = jnp.dot(hidden, down_weight, preferred_element_type=jnp.float32).astype(jnp.bfloat16)
    kept = collect(kept.reshape(mid, far * tokens_here, width), MID).astype(jnp.bfloat16)
    down_sum = collect(kept.reshape(far, tokens_here, width), "zhi")
    return (attended.astype(jnp.float32) + down_sum).astype(jnp.bfloat16)


def on_device(
    queries,
    new_entries,
    resident,
    swap_area,
    swap_dest,
    page_table,
    lengths,
    norm_gain,
    gate_weight,
    up_weight,
    down_weight,
):
    weights = (gate_weight, up_weight, down_weight)
    copies, attended, weights = attention(
        queries, new_entries, resident, swap_area, swap_dest, page_table, lengths, weights
    )
    units = gate_weight.shape[1]
    layer_out = mlp(copies, attended, norm_gain, weights, units)
    return attended.reshape(queries.shape), layer_out.reshape(queries.shape)


def solution(mesh):
    fine = Mesh(mesh.devices.reshape(SIZES), AXES)
    placed = (
        P(ROWS, None, BLK),
        P(ROWS, None, None, BLK),
        P(ROWS, None, None, BLK),
        P(ROWS, None, None, BLK),
        P(ROWS),
        P(ROWS, None),
        P(ROWS),
        P(BLK),
        P(BLK, ROWS),
        P(BLK, ROWS),
        P(ROWS, BLK),
    )
    return jax.shard_map(
        on_device,
        mesh=fine,
        in_specs=placed,
        out_specs=(P(ROWS, None, BLK), P(ROWS, None, BLK)),
        check_vma=False,
    )
```
